128 devices in a mesh: req: 8 (over y, z_lo), ctx: 16 (over x, z_hi, core).
Axes of the slice: x: 4, y: 4, z: 4 (z_hi: 2, z_lo: 2; z = z_hi * 2 + z_lo), core: 2. Of those that a mesh axis runs over, the one named last changes fastest.
Arguments:
- queries: bfloat16 [8, 4096, 4096], P('req', 'ctx'), may hold values from -6 to 6
- kv_new: bfloat16 [8, 2, 4096, 1024], P('req', None, 'ctx'), may hold values from -12 to 12
- kv_pool: bfloat16 [512, 2, 32, 1024], P(('req', 'ctx')), may hold values from -12 to 12
- prefix_pages: int32 [8], P('req'), may hold values from 32 to 64
- reader_owner: int32 [8, 16, 4], P('req', 'ctx'), may hold values from -1 to 7, as said below
- send_page: int32 [8, 16, 8], P('req', 'ctx'), may hold values from -1 to 3, as said below
- tile_doc: int32 [8, 32], P('req'), may hold values from 0 to 8, as said below
Outputs:
- attended: bfloat16 [8, 4096, 4096], P('req', 'ctx')
The draws below stay inside these ranges and needn't reach their ends.
Inputs may be any that keep to these rules, and one draw needn't show every extreme that they name: reader_owner[g, c, i] is -1 exactly where i * 16 + c >= prefix_pages[g]; the entries that are not -1 in one row [g, c] are different groups. send_page[o, c, g] is -1 exactly where reader_owner[g, c] does not name o, else a page number within device c of group o. tile_doc[g] never falls along the tiles; each document number covers 1 to 16 neighbouring tiles.
All inputs are finite; a program needn't handle non-finite values.
Results may differ from the reference program's by a relative error of at most 0.006.
Values may be sent and summed in bfloat16 or wider, within the bound.
A program may use at most 64 MiB of HBM per device.

```python
import math
import jax
import jax.numpy as jnp
from jax import lax

HQ = 32
KEY_VALUE_HEADS = 8
HEAD_SIZE = 128
TILE_POSITIONS = 128
PAGE = 32
PP = 4
POOL_DEV = 4
REQUEST_COUNT = 8
NEW_POSITIONS = 4096
KVW = 1024
QUERY_PER_KEY = 4
DOC_TILE_COUNT = 32
POOL = 512
N_CTX = 16


def float_law(key, dims_shape, spread):
    unshaped_values = jax.random.normal(key, dims_shape, jnp.float32)
    return unshaped_values * spread


def draw_queries(key, part):
    unshaped_values = jnp.clip(float_law(jax.random.fold_in(key, 31), (REQUEST_COUNT, NEW_POSITIONS, HQ * HEAD_SIZE), 1.25), -6.0, 6.0)
    return unshaped_values.astype(jnp.bfloat16)


def draw_kv_new(key, part):
    spread = jnp.array([2.0, 4.0], jnp.float32).reshape(1, 2, 1, 1)
    unshaped_values = jnp.clip(float_law(jax.random.fold_in(key, 21), (REQUEST_COUNT, 2, NEW_POSITIONS, KVW), spread), -12.0, 12.0)
    return unshaped_values.astype(jnp.bfloat16)


def draw_kv_pool(key, part):
    spread = jnp.array([2.0, 4.0], jnp.float32).reshape(1, 2, 1, 1)
    unshaped_values = jnp.clip(float_law(jax.random.fold_in(key, 41), (POOL, 2, PAGE, KVW), spread), -12.0, 12.0)
    return unshaped_values.astype(jnp.bfloat16)


def page_plan(key):
    starting_key = jax.random.fold_in(key, 101)
    lengths = jax.random.randint(jax.random.fold_in(starting_key, 1), (REQUEST_COUNT,), 2 * N_CTX, PP * N_CTX + 1)
    longest = jax.random.randint(jax.random.fold_in(starting_key, 2), (), 0, REQUEST_COUNT)
    shortest = (longest + 1 + jax.random.randint(jax.random.fold_in(starting_key, 3), (), 0, REQUEST_COUNT - 1)) % REQUEST_COUNT
    lengths = lengths.at[longest].set(PP * N_CTX).at[shortest].set(2 * N_CTX)
    scores_raw = jax.random.randint(jax.random.fold_in(starting_key, 4), (REQUEST_COUNT, N_CTX, REQUEST_COUNT), 0, 4096)
    popular = jax.random.randint(jax.random.fold_in(starting_key, 5), (1, N_CTX, REQUEST_COUNT), 0, 3)
    owner_ids = jnp.arange(REQUEST_COUNT, dtype=jnp.int32)
    ranking = (scores_raw + 2048 * popular) * REQUEST_COUNT + owner_ids
    ranking = ranking.at[0, 0, REQUEST_COUNT - 1].set(20000 * REQUEST_COUNT)
    ranked_values, owners = lax.top_k(ranking, PP)
    slot_ids = jnp.arange(PP, dtype=jnp.int32)
    column_ids = jnp.arange(N_CTX, dtype=jnp.int32)
    live = slot_ids[None, None, :] * N_CTX + column_ids[None, :, None] < lengths[:, None, None]
    reader = jnp.where(live, owners, -1).astype(jnp.int32)
    reads_from = jnp.any(reader[..., None] == owner_ids, axis=2)
    local_page = jax.random.randint(jax.random.fold_in(starting_key, 6), (REQUEST_COUNT, N_CTX, REQUEST_COUNT), 0, POOL_DEV)
    local_page = local_page.at[0, 0, :].set(POOL_DEV - 1)
    sent_by = jnp.where(reads_from, local_page, -1)
    sender = jnp.transpose(sent_by, (2, 1, 0)).astype(jnp.int32)
    return (lengths.astype(jnp.int32), reader, sender)


def draw_prefix_pages(key, part):
    return page_plan(key)[0]


def draw_reader_owner(key, part):
    return page_plan(key)[1]


def draw_send_page(key, part):
    return page_plan(key)[2]


def one_document_plan(key):
    longest_doc = DOC_TILE_COUNT // 2
    small_docs = DOC_TILE_COUNT // 4
    rest_tiles = DOC_TILE_COUNT - longest_doc
    cut_order = jax.random.permutation(jax.random.fold_in(key, 1), rest_tiles - 1) + 1
    cut_points = jnp.sort(cut_order[:small_docs - 1]).astype(jnp.int32)
    bounds = jnp.concatenate([jnp.zeros((1,), jnp.int32), cut_points, jnp.full((1,), rest_tiles, jnp.int32)])
    small_lengths = bounds[1:] - bounds[:-1]
    where_long = jax.random.randint(jax.random.fold_in(key, 2), (), 0, small_docs + 1)
    doc_ids = jnp.arange(small_docs + 1, dtype=jnp.int32)
    padded = jnp.concatenate([small_lengths, jnp.zeros((1,), jnp.int32)])
    shifted = jnp.concatenate([jnp.zeros((1,), jnp.int32), small_lengths])
    all_lengths = jnp.where(doc_ids < where_long, padded, jnp.where(doc_ids == where_long, longest_doc, shifted)).astype(jnp.int32)
    doc_ends = jnp.cumsum(all_lengths).astype(jnp.int32)
    tile_ids = jnp.arange(DOC_TILE_COUNT, dtype=jnp.int32)
    return jnp.sum((doc_ends[None, :] <= tile_ids[:, None]).astype(jnp.int32), axis=1).astype(jnp.int32)


def draw_tile_doc(key, part):
    starting_key = jax.random.fold_in(key, 211)
    request_keys = jax.random.split(starting_key, REQUEST_COUNT)
    return jax.vmap(one_document_plan)(request_keys).astype(jnp.int32)


def setup_inputs(seed: int = 0) -> dict:
    keys = jax.random.split(jax.random.key(seed), 8)
    return {
        "queries": draw_queries(jax.random.fold_in(keys[7], 71), 0),
        "kv_new": draw_kv_new(jax.random.fold_in(keys[7], 71), 0),
        "kv_pool": draw_kv_pool(jax.random.fold_in(keys[7], 71), 0),
        "prefix_pages": draw_prefix_pages(jax.random.fold_in(keys[7], 71), 0),
        "reader_owner": draw_reader_owner(jax.random.fold_in(keys[7], 71), 0),
        "send_page": draw_send_page(jax.random.fold_in(keys[7], 71), 0),
        "tile_doc": draw_tile_doc(jax.random.fold_in(keys[7], 71), 0),
    }


def reference(queries, kv_new, kv_pool, prefix_pages, reader_owner, send_page, tile_doc):
    columns = jnp.arange(N_CTX, dtype=jnp.int32)
    safe_owner = jnp.maximum(reader_owner, 0)
    requests = jnp.arange(REQUEST_COUNT, dtype=jnp.int32)[:, None, None]
    local_page = send_page[safe_owner, columns[None, :, None], requests]
    page_id = (safe_owner * N_CTX + columns[None, :, None]) * POOL_DEV + jnp.maximum(local_page, 0)
    page_id = jnp.transpose(page_id, (0, 2, 1)).reshape(REQUEST_COUNT, PP * N_CTX)
    page_live = jnp.arange(PP * N_CTX, dtype=jnp.int32)[None, :] < prefix_pages[:, None]
    positions = jnp.arange(NEW_POSITIONS, dtype=jnp.int32)
    score_scale = 1.0 / math.sqrt(HEAD_SIZE)

    def one_request(single_request):
        page_rows = kv_pool[page_id[single_request]]
        prefix_kv = jnp.transpose(page_rows, (1, 0, 2, 3)).reshape(2, PP * N_CTX * PAGE, KVW)
        all_kv = jnp.concatenate([kv_new[single_request], prefix_kv], axis=1)
        tile_docs = tile_doc[single_request][positions // TILE_POSITIONS]
        new_visible = (positions[None, :] <= positions[:, None]) & (tile_docs[None, :] == tile_docs[:, None])
        prefix_visible = jnp.repeat(page_live[single_request], PAGE)
        visible = jnp.concatenate([new_visible, jnp.broadcast_to(prefix_visible[None, :], (NEW_POSITIONS, PP * N_CTX * PAGE))], axis=1)
        query_head_rows = queries[single_request].reshape(NEW_POSITIONS, KEY_VALUE_HEADS, QUERY_PER_KEY, HEAD_SIZE)

        def single_head(kv_head):
            head_queries = lax.dynamic_index_in_dim(query_head_rows, kv_head, 1, keepdims=False).astype(jnp.float32)
            head_keys = lax.dynamic_slice_in_dim(all_kv[0], kv_head * HEAD_SIZE, HEAD_SIZE, 1).astype(jnp.float32)
            head_values = lax.dynamic_slice_in_dim(all_kv[1], kv_head * HEAD_SIZE, HEAD_SIZE, 1).astype(jnp.float32)
            scores = jnp.einsum('sgd,kd->gsk', head_queries, head_keys) * score_scale
            scores = jnp.where(visible[None], scores, -jnp.inf)
            row_max = lax.optimization_barrier(jnp.max(scores, axis=-1, keepdims=True))
            weights = jnp.where(visible[None], jnp.exp(scores - row_max), 0.0)
            denominator = lax.optimization_barrier(jnp.sum(weights, axis=-1))
            rounded = lax.optimization_barrier(weights.astype(jnp.bfloat16)).astype(jnp.float32)
            summed = jnp.einsum('gsk,kd->sgd', rounded, head_values)
            return summed / jnp.transpose(denominator, (1, 0))[:, :, None]
        output_rows = lax.map(single_head, jnp.arange(KEY_VALUE_HEADS, dtype=jnp.int32))
        return jnp.transpose(output_rows, (1, 0, 2, 3)).reshape(NEW_POSITIONS, HQ * HEAD_SIZE).astype(jnp.bfloat16)
    return lax.map(one_request, jnp.arange(REQUEST_COUNT, dtype=jnp.int32))
```

```python
import functools
import math

import jax
import jax.numpy as jnp
from jax import lax
from jax.experimental import pallas as pl
from jax.experimental.pallas import tpu as pltpu
from jax.sharding import PartitionSpec as P

HEAD = 128
TILE = 128
QROWS = 256
CHUNK = 512
FILL = -1e30
SCALE = math.log2(math.e) / math.sqrt(HEAD)


def scores_of(queries, keys):
    return lax.dot_general(
        queries, keys, (((1,), (1,)), ((), ())), preferred_element_type=jnp.float32
    )


def attend_kernel(info, q_ref, new_ref, pre_ref, out_ref):
    block = pl.program_id(0)
    pages = info[0]
    heads = q_ref.shape[1] // HEAD
    rows = heads * QROWS
    page_rows = pre_ref.shape[1] // 64
    queries = jnp.concatenate(
        [q_ref[:, h * HEAD : (h + 1) * HEAD] for h in range(heads)], axis=0
    )

    def fold(state, scores, values):
        top, total, acc = state
        new_top = jnp.maximum(top, jnp.max(scores, axis=1, keepdims=True))
        weights = jnp.exp2((scores - new_top) * SCALE)
        rescale = jnp.exp2((top - new_top) * SCALE)
        total = total * rescale + jnp.sum(weights, axis=1, keepdims=True)
        acc = acc * rescale + jnp.dot(
            weights.astype(jnp.bfloat16), values, preferred_element_type=jnp.float32
        )
        return new_top, total, acc

    first = 32 * page_rows
    scores = scores_of(queries, pre_ref[0, :first, :])
    top = jnp.max(scores, axis=1, keepdims=True)
    weights = jnp.exp2((scores - top) * SCALE)
    total = jnp.sum(weights, axis=1, keepdims=True)
    acc = jnp.dot(
        weights.astype(jnp.bfloat16), pre_ref[1, :first, :], preferred_element_type=jnp.float32
    )
    state = (top, total, acc)

    def prefix_step(i, state):
        at = pl.multiple_of(i * CHUNK, CHUNK)
        scores = scores_of(queries, pre_ref[0, pl.ds(at, CHUNK), :])
        column = lax.broadcasted_iota(jnp.int32, scores.shape, 1)
        scores = jnp.where(column < pages * page_rows - at, scores, FILL)
        return fold(state, scores, pre_ref[1, pl.ds(at, CHUNK), :])

    live = pages * page_rows
    state = lax.fori_loop(first // CHUNK, (live + CHUNK - 1) // CHUNK, prefix_step, state)

    per = QROWS // TILE
    row = lax.broadcasted_iota(jnp.int32, (rows, 1), 0) % QROWS
    low = jnp.full((rows, 1), info[1 + block * per] * TILE, jnp.int32)
    for t in range(1, per):
        low = jnp.where(row >= t * TILE, info[1 + block * per + t] * TILE, low)
    position = row + block * QROWS

    def new_step(i, state):
        at = pl.multiple_of(i * QROWS, QROWS)
        scores = scores_of(queries, new_ref[0, pl.ds(at, QROWS), :])
        column = lax.broadcasted_iota(jnp.int32, scores.shape, 1) + at
        scores = jnp.where((column >= low) & (column <= position), scores, FILL)
        return fold(state, scores, new_ref[1, pl.ds(at, QROWS), :])

    state = lax.fori_loop(info[1 + block * per] // per, block + 1, new_step, state)
    _, total, acc = state
    result = (acc / total).astype(out_ref.dtype)
    for h in range(heads):
        out_ref[:, h * HEAD : (h + 1) * HEAD] = result[h * QROWS : (h + 1) * QROWS]


def attend(info, queries, new_kv, prefix_kv):
    positions, width = queries.shape
    whole = lambda shape: pl.BlockSpec(shape, lambda i, s: (0,) * len(shape))
    return pl.pallas_call(
        attend_kernel,
        out_shape=jax.ShapeDtypeStruct((positions, width), queries.dtype),
        grid_spec=pltpu.PrefetchScalarGridSpec(
            num_scalar_prefetch=1,
            grid=(positions // QROWS,),
            in_specs=[
                pl.BlockSpec((QROWS, width), lambda i, s: (i, 0)),
                whole(new_kv.shape),
                whole(prefix_kv.shape),
            ],
            out_specs=pl.BlockSpec((QROWS, width), lambda i, s: (i, 0)),
        ),
        compiler_params=pltpu.CompilerParams(
            dimension_semantics=("arbitrary",), vmem_limit_bytes=48 << 20
        ),
        cost_estimate=pl.CostEstimate(
            flops=4 * positions * width * 2560, bytes_accessed=10 << 20, transcendentals=0
        ),
        name="attend",
    )(info, queries, new_kv, prefix_kv)


def pick(pages, ids):
    return jnp.stack(
        [
            lax.dynamic_index_in_dim(pages, jnp.maximum(ids[i], 0), 0, keepdims=False)
            for i in range(ids.shape[0])
        ]
    )


def local(queries, kv_new, kv_pool, prefix_pages, reader_owner, send_page, tile_doc):
    columns = lax.axis_size("ctx")
    kv_heads = kv_new.shape[3] // HEAD
    page_len = kv_pool.shape[2]
    slots = reader_owner.shape[2]
    copies = columns // kv_heads
    wanted = send_page[0, 0]
    outgoing = pick(kv_pool, wanted)
    arrived = lax.all_to_all(outgoing, "req", split_axis=0, concat_axis=0, tiled=True)
    prefix_kv = pick(arrived, reader_owner[0, 0])
    prefix_kv = jnp.transpose(prefix_kv, (1, 0, 2, 3)).reshape(2, slots * page_len, -1)
    block = jnp.concatenate([kv_new[0], prefix_kv], axis=1)
    block = block.reshape(2, -1, kv_heads, HEAD)
    block = jnp.repeat(jnp.transpose(block, (2, 0, 1, 3)), copies, axis=0)
    kv = lax.all_to_all(block, "ctx", split_axis=0, concat_axis=0, tiled=True)
    rows = kv_new.shape[2]
    new_kv = jnp.transpose(kv[:, :, :rows], (1, 0, 2, 3)).reshape(2, -1, HEAD)
    pre = kv[:, :, rows:].reshape(columns, 2, slots, page_len, HEAD)
    pre = jnp.transpose(pre, (1, 2, 0, 3, 4)).reshape(2, -1, HEAD)
    q = lax.all_to_all(queries[0], "ctx", split_axis=1, concat_axis=0, tiled=True)
    docs = tile_doc[0]
    starts = jnp.sum((docs[None, :] < docs[:, None]).astype(jnp.int32), axis=1)
    info = jnp.concatenate([prefix_pages, starts])
    out = attend(info, q, new_kv, pre)
    out = lax.all_to_all(out, "ctx", split_axis=0, concat_axis=1, tiled=True)
    return out[None]


def solution(mesh):
    in_specs = (
        P("req", "ctx", None),
        P("req", None, "ctx", None),
        P(("req", "ctx"), None, None, None),
        P("req"),
        P("req", "ctx", None),
        P("req", "ctx", None),
        P("req", None),
    )
    return jax.shard_map(
        local, mesh=mesh, in_specs=in_specs, out_specs=P("req", "ctx", None), check_vma=False
    )
```

```python
import math

import jax
import jax.numpy as jnp
from jax import lax
from jax.experimental import pallas as pl
from jax.experimental.pallas import tpu as pltpu
from jax.sharding import PartitionSpec as P

HEAD = 128
TILE = 128
FILL = -1e30
SCALE = math.log2(math.e) / math.sqrt(HEAD)
MESH = pl.DeviceIdType.MESH


def scores_of(queries, keys):
    return lax.dot_general(
        queries, keys, (((1,), (1,)), ((), ())), preferred_element_type=jnp.float32
    )


def decay(scores, top):
    return jnp.exp2((scores - top) * SCALE)


def gather_kernel(
    columns, groups, wanted, owners, pool, q_ref, new_ref, q_all, kv_all, pre_all,
    outgoing, arrived, staged, req_send, req_recv, q_send, q_recv, kv_send, kv_recv,
    kv_pass, pre_send, pre_recv, pre_pass, near,
):
    me = lax.axis_index("ctx")
    group = lax.axis_index("req")
    chips = columns // 2
    chip = me // 2
    core = me % 2
    sibling = chip * 2 + (1 - core)
    rows = q_ref.shape[0]
    width = q_all.shape[1]

    barrier = pltpu.get_barrier_semaphore()

    def greet_column(t, c):
        pl.semaphore_signal(
            barrier, inc=1, device_id={"ctx": (me + t) % columns}, device_id_type=MESH
        )
        return c

    def greet_group(t, c):
        pl.semaphore_signal(
            barrier, inc=1, device_id={"req": (group + t) % groups}, device_id_type=MESH
        )
        return c

    lax.fori_loop(1, columns, greet_column, 0)
    lax.fori_loop(1, groups, greet_group, 0)
    for g in range(groups):
        outgoing[g] = pool[jnp.maximum(wanted[0, 0, g], 0)]
    arrived[group] = outgoing[group]
    pl.semaphore_wait(barrier, columns + groups - 2)

    def page_copy(t):
        to = (group + t) % groups
        return pltpu.make_async_remote_copy(
            outgoing.at[to], arrived.at[group], req_send.at[t], req_recv.at[group],
            device_id={"req": to}, device_id_type=MESH,
        )

    def q_copy(t):
        to = (me + t) % columns
        return pltpu.make_async_remote_copy(
            q_ref.at[:, pl.ds(pl.multiple_of(to * width, width), width)],
            q_all.at[pl.ds(pl.multiple_of(me * rows, rows), rows), :],
            q_send.at[t], q_recv.at[me], device_id={"ctx": to}, device_id_type=MESH,
        )

    def kv_slot(source):
        return kv_all.at[:, pl.ds(pl.multiple_of(source * rows, rows), rows), :]

    def head(ref, at):
        cut = pl.ds(pl.multiple_of(at * HEAD, HEAD), HEAD)
        return ref.at[:, :, cut] if len(ref.shape) == 3 else ref.at[:, :, :, cut]

    def kv_copy(t):
        to = (chip + t) % chips
        return pltpu.make_async_remote_copy(
            head(new_ref, to), kv_slot(me), kv_send.at[t], kv_recv.at[me],
            device_id={"ctx": to * 2 + core}, device_id_type=MESH,
        )

    def pre_copy(t):
        to = (chip + t) % chips
        return pltpu.make_async_remote_copy(
            head(staged, to), pre_all.at[:, :, me], pre_send.at[t], pre_recv.at[me],
            device_id={"ctx": to * 2 + core}, device_id_type=MESH,
        )

    def source_of(t):
        return ((chip + chips - t) % chips) * 2 + core

    def kv_onward(t):
        slot = kv_slot(source_of(t))
        return pltpu.make_async_remote_copy(
            slot, slot, kv_pass.at[t], kv_recv.at[source_of(t)],
            device_id={"ctx": sibling}, device_id_type=MESH,
        )

    def pre_onward(t):
        slot = pre_all.at[:, :, source_of(t)]
        return pltpu.make_async_remote_copy(
            slot, slot, pre_pass.at[t], pre_recv.at[source_of(t)],
            device_id={"ctx": sibling}, device_id_type=MESH,
        )

    def kv_twin():
        return pltpu.make_async_remote_copy(
            head(new_ref, chip), kv_slot(me), kv_pass.at[0], kv_recv.at[me],
            device_id={"ctx": sibling}, device_id_type=MESH,
        )

    def pre_twin():
        return pltpu.make_async_remote_copy(
            head(staged, chip), pre_all.at[:, :, me], pre_pass.at[0], pre_recv.at[me],
            device_id={"ctx": sibling}, device_id_type=MESH,
        )

    own = [
        pltpu.make_async_copy(
            q_ref.at[:, pl.ds(pl.multiple_of(me * width, width), width)],
            q_all.at[pl.ds(pl.multiple_of(me * rows, rows), rows), :],
            near.at[0],
        ),
        pltpu.make_async_copy(head(new_ref, chip), kv_slot(me), near.at[1]),
        pltpu.make_async_copy(head(staged, chip), pre_all.at[:, :, me], near.at[2]),
    ]

    def each(count, act, first=1):
        def step(t, c):
            act(t)
            return c

        lax.fori_loop(first, count, step, 0)

    each(groups, lambda t: page_copy(t).start())
    each(chips, lambda t: kv_copy(t).start())
    each(columns, lambda t: q_copy(t).start())
    kv_twin().start()
    own[0].start()
    own[1].start()

    def page_arrival(t):
        source = (group + groups - t) % groups
        pltpu.make_async_remote_copy(
            outgoing.at[source], arrived.at[source], req_send.at[0], req_recv.at[source],
            device_id={"req": source}, device_id_type=MESH,
        ).wait_recv()

    each(groups, page_arrival)
    for i in range(staged.shape[1]):
        page = arrived[jnp.maximum(owners[0, 0, i], 0)]
        staged[:, i] = page
    each(chips, lambda t: pre_copy(t).start())
    pre_twin().start()
    own[2].start()

    def kv_relay(t):
        kv_onward(t).wait_recv()
        kv_onward(t).start()

    def pre_relay(t):
        pre_onward(t).wait_recv()
        pre_onward(t).start()

    each(chips, kv_relay)
    each(chips, pre_relay)

    def q_arrival(t):
        source = (me + columns - t) % columns
        pltpu.make_async_remote_copy(
            q_all.at[pl.ds(pl.multiple_of(source * rows, rows), rows), :],
            q_all.at[pl.ds(pl.multiple_of(source * rows, rows), rows), :],
            q_send.at[0], q_recv.at[source], device_id={"ctx": source}, device_id_type=MESH,
        ).wait_recv()

    each(columns, q_arrival)

    def twin_arrival(t):
        source = ((chip + t) % chips) * 2 + (1 - core)
        for slot, sem in ((kv_slot(source), kv_recv), (pre_all.at[:, :, source], pre_recv)):
            pltpu.make_async_remote_copy(
                slot, slot, near.at[3], sem.at[source],
                device_id={"ctx": sibling}, device_id_type=MESH,
            ).wait_recv()

    each(chips, twin_arrival, 0)
    each(groups, lambda t: page_copy(t).wait_send())
    each(columns, lambda t: q_copy(t).wait_send())
    each(chips, lambda t: kv_copy(t).wait_send())
    each(chips, lambda t: pre_copy(t).wait_send())
    each(chips, lambda t: kv_onward(t).wait_send())
    each(chips, lambda t: pre_onward(t).wait_send())
    kv_twin().wait_send()
    pre_twin().wait_send()
    for copy in own:
        copy.wait()


def gather(wanted, owners, pool, queries, kv_new, columns, groups):
    rows, features = queries.shape
    slots, page_len = owners.shape[2], pool.shape[2]
    dtype = queries.dtype
    dma = pltpu.SemaphoreType.DMA
    anywhere = pl.BlockSpec(memory_space=pl.ANY)
    chips = columns // 2
    return pl.pallas_call(
        lambda *refs: gather_kernel(columns, groups, *refs),
        out_shape=(
            jax.ShapeDtypeStruct((rows * columns, features // columns), dtype),
            jax.ShapeDtypeStruct((2, rows * columns, HEAD), dtype),
            jax.ShapeDtypeStruct((2, slots, columns, page_len, HEAD), dtype),
        ),
        in_specs=[
            pl.BlockSpec(memory_space=pltpu.SMEM),
            pl.BlockSpec(memory_space=pltpu.SMEM),
            pl.BlockSpec(memory_space=pltpu.VMEM),
            anywhere,
            anywhere,
        ],
        out_specs=(anywhere, anywhere, anywhere),
        scratch_shapes=[
            pltpu.VMEM((groups,) + pool.shape[1:], dtype),
            pltpu.VMEM((groups,) + pool.shape[1:], dtype),
            pltpu.VMEM((2, slots) + pool.shape[2:], dtype),
            dma((groups,)), dma((groups,)),
            dma((columns,)), dma((columns,)),
            dma((chips,)), dma((columns,)), dma((chips,)),
            dma((chips,)), dma((columns,)), dma((chips,)),
            dma((4,)),
        ],
        compiler_params=pltpu.CompilerParams(
            collective_id=0, has_side_effects=True, vmem_limit_bytes=16 << 20
        ),
        name="gather",
    )(wanted, owners, pool, queries, kv_new)


def new_kernel(info, q_ref, kv_ref, acc_ref, stat_ref):
    block = pl.program_id(0)
    rows, width = q_ref.shape
    heads = width // HEAD
    per = rows // TILE
    row = lax.broadcasted_iota(jnp.int32, (rows, 1), 0)
    low = jnp.full((rows, 1), info[block * per] * TILE, jnp.int32)
    for t in range(1, per):
        low = jnp.where(row >= t * TILE, info[block * per + t] * TILE, low)
    position = row + block * rows
    queries = [q_ref[:, h * HEAD : (h + 1) * HEAD] for h in range(heads)]

    def visible(at, size, last):
        column = lax.broadcasted_iota(jnp.int32, (rows, size), 1) + at
        seen = column >= low
        return seen & (column <= position) if last else seen

    def fold(at, size, states):
        keys, values = kv_ref[0, pl.ds(at, size), :], kv_ref[1, pl.ds(at, size), :]
        seen = visible(at, size, states is None)
        result = []
        for h in range(heads):
            scores = jnp.where(seen, scores_of(queries[h], keys), FILL)
            top = jnp.max(scores, axis=1, keepdims=True)
            if states is not None:
                top = jnp.maximum(top, states[h][0])
            weights = decay(scores, top)
            total = jnp.sum(weights, axis=1, keepdims=True)
            acc = jnp.dot(
                weights.astype(jnp.bfloat16), values, preferred_element_type=jnp.float32
            )
            if states is not None:
                shrink = decay(states[h][0], top)
                total = total + states[h][1] * shrink
                acc = acc + states[h][2] * shrink
            result.append((top, total, acc))
        return tuple(result)

    def whole(index):
        return pl.multiple_of(index * rows, rows)

    begin = info[block * per] // per
    count = block - begin
    states = fold(whole(block), rows, None)
    states = lax.fori_loop(
        0, count // 4, lambda i, s: fold(whole(begin + i * 4), 4 * rows, s), states
    )
    states = lax.cond(
        count % 4 >= 2, lambda s: fold(whole(block - count % 4), 2 * rows, s), lambda s: s, states
    )
    states = lax.cond(count % 2 == 1, lambda s: fold(whole(block - 1), rows, s), lambda s: s, states)
    lane = lax.broadcasted_iota(jnp.int32, stat_ref.shape, 1)
    stat = jnp.zeros(stat_ref.shape, jnp.float32)
    for h in range(heads):
        acc_ref[:, h * HEAD : (h + 1) * HEAD] = states[h][2]
        stat = jnp.where(lane == 2 * h, states[h][0], stat)
        stat = jnp.where(lane == 2 * h + 1, states[h][1], stat)
    stat_ref[...] = stat


def attend_new(starts, queries, kv, rows):
    positions, width = queries.shape
    return pl.pallas_call(
        new_kernel,
        out_shape=(
            jax.ShapeDtypeStruct((positions, width), jnp.float32),
            jax.ShapeDtypeStruct((positions, HEAD), jnp.float32),
        ),
        grid_spec=pltpu.PrefetchScalarGridSpec(
            num_scalar_prefetch=1,
            grid=(positions // rows,),
            in_specs=[
                pl.BlockSpec((rows, width), lambda i, s: (i, 0)),
                pl.BlockSpec(kv.shape, lambda i, s: (0, 0, 0)),
            ],
            out_specs=(
                pl.BlockSpec((rows, width), lambda i, s: (i, 0)),
                pl.BlockSpec((rows, HEAD), lambda i, s: (i, 0)),
            ),
        ),
        compiler_params=pltpu.CompilerParams(
            dimension_semantics=("arbitrary",), vmem_limit_bytes=32 << 20
        ),
        name="attend_new",
    )(starts, queries, kv)


def finish_kernel(
    columns, pages, q_ref, pre_ref, acc_ref, stat_ref, out_ref, stage, send, recv, near
):
    me = lax.axis_index("ctx")
    positions, width = q_ref.shape
    rows = positions // columns
    heads = width // HEAD
    keys = pre_ref.shape[1]

    barrier = pltpu.get_barrier_semaphore()

    def greet(t, c):
        pl.semaphore_signal(
            barrier, inc=1, device_id={"ctx": (me + t) % columns}, device_id_type=MESH
        )
        return c

    lax.fori_loop(1, columns, greet, 0)
    pl.semaphore_wait(barrier, columns - 1)
    live = pages[0] * (keys // 64)

    def compute(block):
        at = pl.ds(pl.multiple_of(block * rows, rows), rows)
        for h in range(heads):
            cut = slice(h * HEAD, (h + 1) * HEAD)
            scores = scores_of(q_ref[at, cut], pre_ref[0])
            half = keys // 2
            column = lax.broadcasted_iota(jnp.int32, (rows, half), 1) + half
            scores = jnp.concatenate(
                [scores[:, :half], jnp.where(column < live, scores[:, half:], FILL)], axis=1
            )
            before = stat_ref[at, 2 * h : 2 * h + 1]
            top = jnp.maximum(jnp.max(scores, axis=1, keepdims=True), before)
            weights = decay(scores, top)
            shrink = decay(before, top)
            total = jnp.sum(weights, axis=1, keepdims=True)
            total = total + stat_ref[at, 2 * h + 1 : 2 * h + 2] * shrink
            acc = jnp.dot(
                weights.astype(jnp.bfloat16), pre_ref[1], preferred_element_type=jnp.float32
            )
            acc = acc + acc_ref[at, cut] * shrink
            stage[at, cut] = (acc / total).astype(stage.dtype)

    def cut_of(device):
        return out_ref.at[:, pl.ds(pl.multiple_of(device * width, width), width)]

    def staged(block):
        return stage.at[pl.ds(pl.multiple_of(block * rows, rows), rows), :]

    def out_copy(t):
        to = (me + t) % columns
        return pltpu.make_async_remote_copy(
            staged(to), cut_of(me), send.at[t], recv.at[me],
            device_id={"ctx": to}, device_id_type=MESH,
        )

    def step(i, c):
        t = columns - 1 - i
        compute((me + t) % columns)
        out_copy(t).start()
        return c

    lax.fori_loop(0, columns - 1, step, 0)
    compute(me)
    mine = pltpu.make_async_copy(staged(me), cut_of(me), near)
    mine.start()

    def settle(t, c):
        source = (me + t) % columns
        pltpu.make_async_remote_copy(
            staged(source), cut_of(source), send.at[0], recv.at[source],
            device_id={"ctx": source}, device_id_type=MESH,
        ).wait_recv()
        out_copy(t).wait_send()
        return c

    lax.fori_loop(1, columns, settle, 0)
    mine.wait()


def finish(pages, queries, pre, acc, stat, columns):
    positions, width = queries.shape
    vmem = pl.BlockSpec(memory_space=pltpu.VMEM)
    return pl.pallas_call(
        lambda *refs: finish_kernel(columns, *refs),
        out_shape=jax.ShapeDtypeStruct((positions // columns, width * columns), queries.dtype),
        in_specs=[pl.BlockSpec(memory_space=pltpu.SMEM), vmem, vmem, vmem, vmem],
        out_specs=pl.BlockSpec(memory_space=pl.ANY),
        scratch_shapes=[
            pltpu.VMEM((positions, width), queries.dtype),
            pltpu.SemaphoreType.DMA((columns,)),
            pltpu.SemaphoreType.DMA((columns,)),
            pltpu.SemaphoreType.DMA,
        ],
        compiler_params=pltpu.CompilerParams(
            collective_id=1, has_side_effects=True, vmem_limit_bytes=40 << 20
        ),
        name="finish",
    )(pages, queries, pre, acc, stat)


def local(queries, kv_new, kv_pool, prefix_pages, reader_owner, send_page, tile_doc):
    columns, groups = lax.axis_size("ctx"), lax.axis_size("req")
    rows = queries.shape[1]
    q, kv, pre = gather(
        send_page, reader_owner, kv_pool, queries[0], kv_new[0], columns, groups
    )
    pre = pre.reshape(2, -1, HEAD)
    docs = tile_doc[0]
    starts = jnp.sum((docs[None, :] < docs[:, None]).astype(jnp.int32), axis=1)
    acc, stat = attend_new(starts, q, kv, rows)
    return finish(prefix_pages, q, pre, acc, stat, columns)[None]


def solution(mesh):
    in_specs = (
        P("req", "ctx", None),
        P("req", None, "ctx", None),
        P(("req", "ctx"), None, None, None),
        P("req"),
        P("req", "ctx", None),
        P("req", "ctx", None),
        P("req", None),
    )
    return jax.shard_map(
        local, mesh=mesh, in_specs=in_specs, out_specs=P("req", "ctx", None), check_vma=False
    )
```

```python
import math

import jax
import jax.numpy as jnp
from jax import lax
from jax.experimental import pallas as pl
from jax.experimental.pallas import tpu as pltpu
from jax.sharding import PartitionSpec as P

HEAD = 128
TILE = 128
FILL = -1e30
SCALE = math.log2(math.e) / math.sqrt(HEAD)
MESH = pl.DeviceIdType.MESH
EARLY = 10
FIRST = 4


def scores_of(queries, keys):
    return lax.dot_general(
        queries, keys, (((1,), (1,)), ((), ())), preferred_element_type=jnp.float32
    )


def decay(scores, top):
    return jnp.exp2((scores - top) * SCALE)


def prefix_part(queries, pre_ref, live):
    keys = pre_ref.shape[1]
    half = keys // 2
    scores = scores_of(queries, pre_ref[0])
    column = lax.broadcasted_iota(jnp.int32, (queries.shape[0], half), 1) + half
    scores = jnp.concatenate(
        [scores[:, :half], jnp.where(column < live, scores[:, half:], FILL)], axis=1
    )
    top = jnp.max(scores, axis=1, keepdims=True)
    weights = decay(scores, top)
    total = jnp.sum(weights, axis=1, keepdims=True)
    acc = jnp.dot(weights.astype(jnp.bfloat16), pre_ref[1], preferred_element_type=jnp.float32)
    return top, total, acc


def joined(one, two):
    top = jnp.maximum(one[0], two[0])
    left, right = decay(one[0], top), decay(two[0], top)
    return top, one[1] * left + two[1] * right, one[2] * left + two[2] * right


def pack(tops_and_totals):
    shape = (tops_and_totals[0].shape[0], HEAD)
    lane = lax.broadcasted_iota(jnp.int32, shape, 1)
    stat = jnp.zeros(shape, jnp.float32)
    for at, column in enumerate(tops_and_totals):
        stat = jnp.where(lane == at, column, stat)
    return stat


def part_of(acc_ref, stat_ref, at, h):
    return (
        stat_ref[at, 2 * h : 2 * h + 1],
        stat_ref[at, 2 * h + 1 : 2 * h + 2],
        acc_ref[at, h * HEAD : (h + 1) * HEAD],
    )


def span(index, size):
    start = index * size
    return pl.ds(start if isinstance(start, int) else pl.multiple_of(start, size), size)


def partner(me, r, columns, sends):
    chips_x = columns // 4
    x, z, core = me // 4, (me // 2) % 2, me % 2
    x = (x + r // 4) % chips_x if sends else (x + chips_x - r // 4) % chips_x
    return x * 4 + ((z + r) % 2) * 2 + (core + r // 2) % 2


def partner_chip(chip, t, chips, sends):
    chips_x = chips // 2
    x, z = chip // 2, chip % 2
    x = (x + t // 2) % chips_x if sends else (x + chips_x - t // 2) % chips_x
    return x * 2 + (z + t) % 2


def each(first, last, act):
    def step(t, c):
        act(t)
        return c

    lax.fori_loop(first, last, step, 0)


def gather_kernel(
    columns, groups, early, wanted, owners, pages, pool_ref, q_ref, new_ref,
    q_all, kv_all, pre_all, acc_ref, stat_ref,
    pool, outgoing, arrived, staged, req_send, req_recv, q_send, q_recv, kv_send, kv_recv,
    kv_pass, pre_send, pre_recv, pre_pass, near,
):
    me = lax.axis_index("ctx")
    group = lax.axis_index("req")
    chips = columns // 2
    chip = me // 2
    core = me % 2
    sibling = chip * 2 + (1 - core)
    rows = q_ref.shape[0]
    width = q_all.shape[1]
    heads = width // HEAD
    slots, page_len = staged.shape[1], staged.shape[2]
    first = FIRST
    pool_copy = pltpu.make_async_copy(pool_ref, pool, near.at[3])
    pool_copy.start()

    barrier = pltpu.get_barrier_semaphore()

    def greet_column(r):
        to = partner(me, r, columns, True)
        pl.semaphore_signal(barrier, inc=1, device_id={"ctx": to}, device_id_type=MESH)

    def greet_group(t):
        to = (group + t) % groups
        pl.semaphore_signal(barrier, inc=1, device_id={"req": to}, device_id_type=MESH)

    each(1, groups, greet_group)
    each(1, columns, greet_column)
    pool_copy.wait()
    for g in range(groups):
        outgoing[g] = pool[jnp.maximum(wanted[0, 0, g], 0)]
    arrived[group] = outgoing[group]
    pl.semaphore_wait(barrier, columns + groups - 2)

    def page_copy(t):
        to = (group + t) % groups
        return pltpu.make_async_remote_copy(
            outgoing.at[to], arrived.at[group], req_send.at[t], req_recv.at[group],
            device_id={"req": to}, device_id_type=MESH,
        )

    def q_cut(device):
        return q_ref.at[:, span(device, width)]

    def q_slot(device):
        return q_all.at[span(device, rows), :]

    def kv_slot(device):
        return kv_all.at[:, span(device, rows), :]

    def pre_slot(device):
        return pre_all.at[:, :, device]

    def new_cut(at):
        return new_ref.at[:, :, span(at, HEAD)]

    def pre_cut(at):
        return staged.at[:, :, :, span(at, HEAD)]

    def q_copy(r):
        to = partner(me, r, columns, True)
        return pltpu.make_async_remote_copy(
            q_cut(to), q_slot(me), q_send.at[r], q_recv.at[me],
            device_id={"ctx": to}, device_id_type=MESH,
        )

    def kv_copy(t):
        to = partner_chip(chip, t, chips, True)
        return pltpu.make_async_remote_copy(
            new_cut(to), kv_slot(me), kv_send.at[t], kv_recv.at[me],
            device_id={"ctx": to * 2 + core}, device_id_type=MESH,
        )

    def pre_copy(t):
        to = partner_chip(chip, t, chips, True)
        return pltpu.make_async_remote_copy(
            pre_cut(to), pre_slot(me), pre_send.at[t], pre_recv.at[me],
            device_id={"ctx": to * 2 + core}, device_id_type=MESH,
        )

    def source_of(t):
        return partner_chip(chip, t, chips, False) * 2 + core

    def to_sibling(source_ref, slot, send, recv):
        return pltpu.make_async_remote_copy(
            source_ref, slot, send, recv, device_id={"ctx": sibling}, device_id_type=MESH
        )

    def kv_onward(t):
        slot = kv_slot(source_of(t))
        return to_sibling(slot, slot, kv_pass.at[t], kv_recv.at[source_of(t)])

    def pre_onward(t):
        slot = pre_slot(source_of(t))
        return to_sibling(slot, slot, pre_pass.at[t], pre_recv.at[source_of(t)])

    kv_twin = to_sibling(new_cut(chip), kv_slot(me), kv_pass.at[0], kv_recv.at[me])
    pre_twin = to_sibling(pre_cut(chip), pre_slot(me), pre_pass.at[0], pre_recv.at[me])
    own = [
        pltpu.make_async_copy(q_cut(me), q_slot(me), near.at[0]),
        pltpu.make_async_copy(new_cut(chip), kv_slot(me), near.at[1]),
        pltpu.make_async_copy(pre_cut(chip), pre_slot(me), near.at[2]),
    ]

    each(1, groups, lambda t: page_copy(t).start())
    each(1, first, lambda r: q_copy(r).start())
    own[0].start()
    own[1].start()

    def page_arrival(t):
        source = (group + groups - t) % groups
        pltpu.make_async_remote_copy(
            outgoing.at[source], arrived.at[source], req_send.at[0], req_recv.at[source],
            device_id={"req": source}, device_id_type=MESH,
        ).wait_recv()

    each(1, groups, page_arrival)
    for i in range(slots):
        staged[:, i] = arrived[jnp.maximum(owners[0, 0, i], 0)]
    each(1, chips, lambda t: pre_copy(t).start())
    pre_twin.start()
    own[2].start()
    each(first, columns, lambda r: q_copy(r).start())
    each(1, chips, lambda t: kv_copy(t).start())
    kv_twin.start()

    def pre_relay(t):
        pre_onward(t).wait_recv()
        pre_onward(t).start()

    each(1, chips, pre_relay)

    def pre_twin_arrival(t):
        source = partner_chip(chip, t, chips, False) * 2 + (1 - core)
        to_sibling(pre_slot(source), pre_slot(source), near.at[3], pre_recv.at[source]).wait_recv()

    each(0, chips, pre_twin_arrival)
    own[0].wait()
    own[2].wait()
    keys = slots * columns * page_len
    live = pages[0] * page_len
    prefix = pre_all.reshape(2, keys, HEAD)

    def q_arrival(r):
        source = partner(me, r, columns, False)
        pltpu.make_async_remote_copy(
            q_slot(source), q_slot(source), q_send.at[0], q_recv.at[source],
            device_id={"ctx": source}, device_id_type=MESH,
        ).wait_recv()

    def attend(r):
        at = span(partner(me, r, columns, False), rows)
        out = span(r, rows)
        found = []
        for h in range(heads):
            cut = slice(h * HEAD, (h + 1) * HEAD)
            top, total, acc = prefix_part(q_all[at, cut], prefix, live)
            acc_ref[out, cut] = acc
            found += [top, total]
        stat_ref[out, :] = pack(found)

    attend(0)

    def arrive_and_attend(r):
        q_arrival(r)
        attend(r)

    each(1, early, arrive_and_attend)

    def kv_relay(t):
        kv_onward(t).wait_recv()
        kv_onward(t).start()

    each(1, chips, kv_relay)
    each(early, columns, q_arrival)

    def kv_twin_arrival(t):
        source = partner_chip(chip, t, chips, False) * 2 + (1 - core)
        to_sibling(kv_slot(source), kv_slot(source), near.at[3], kv_recv.at[source]).wait_recv()

    each(0, chips, kv_twin_arrival)
    each(1, groups, lambda t: page_copy(t).wait_send())
    each(1, columns, lambda r: q_copy(r).wait_send())
    for copies in (kv_copy, pre_copy, kv_onward, pre_onward):
        each(1, chips, lambda t, copies=copies: copies(t).wait_send())
    kv_twin.wait_send()
    pre_twin.wait_send()
    own[1].wait()


def gather(wanted, owners, pages, pool, queries, kv_new, columns, groups, early):
    rows, features = queries.shape
    slots, page_len = owners.shape[2], pool.shape[2]
    dtype = queries.dtype
    width = features // columns
    dma = pltpu.SemaphoreType.DMA
    smem = pl.BlockSpec(memory_space=pltpu.SMEM)
    vmem = pl.BlockSpec(memory_space=pltpu.VMEM)
    hbm = pl.BlockSpec(memory_space=pltpu.HBM)
    chips = columns // 2
    return pl.pallas_call(
        lambda *refs: gather_kernel(columns, groups, early, *refs),
        out_shape=(
            jax.ShapeDtypeStruct((rows * columns, width), dtype),
            jax.ShapeDtypeStruct((2, rows * columns, HEAD), dtype),
            jax.ShapeDtypeStruct((2, slots, columns, page_len, HEAD), dtype),
            jax.ShapeDtypeStruct((rows * early, width), jnp.float32),
            jax.ShapeDtypeStruct((rows * early, HEAD), jnp.float32),
        ),
        in_specs=[smem, smem, smem, hbm, hbm, hbm],
        out_specs=(vmem, vmem, vmem, vmem, vmem),
        scratch_shapes=[
            pltpu.VMEM(pool.shape, dtype),
            pltpu.VMEM((groups,) + pool.shape[1:], dtype),
            pltpu.VMEM((groups,) + pool.shape[1:], dtype),
            pltpu.VMEM((2, slots) + pool.shape[2:], dtype),
            dma((groups,)), dma((groups,)),
            dma((columns,)), dma((columns,)),
            dma((chips,)), dma((columns,)), dma((chips,)),
            dma((chips,)), dma((columns,)), dma((chips,)),
            dma((4,)),
        ],
        compiler_params=pltpu.CompilerParams(
            collective_id=0, has_side_effects=True, vmem_limit_bytes=32 << 20
        ),
        name="gather",
    )(wanted, owners, pages, pool, queries, kv_new)


def new_kernel(
    early, docs, q_ref, kv_ref, acc_pre, stat_pre, done_ref, acc_ref, stat_ref, acc_s, stat_s, starts
):
    me = lax.axis_index("ctx")
    rows, width = acc_s.shape
    heads = width // HEAD
    per = rows // TILE
    positions = q_ref.shape[0]
    columns = positions // rows
    longest = 16 // per
    starts[0] = 0

    def begin_of(t):
        starts[t] = jnp.where(docs[0, t] == docs[0, t - 1], starts[t - 1], t)

    each(1, columns * per, begin_of)

    def do(slot, c):
        block = partner(me, slot, columns, False)
        begin = starts[block * per] // per
        count = block - begin
        row = lax.broadcasted_iota(jnp.int32, (rows, 1), 0)
        low = jnp.full((rows, 1), starts[block * per] * TILE, jnp.int32)
        for t in range(1, per):
            low = jnp.where(row >= t * TILE, starts[block * per + t] * TILE, low)
        low = low - begin * rows
        at = span(block, rows)

        def fold(before):
            size = (before + 1) * rows
            window = pl.ds(pl.multiple_of(begin * rows, rows), size)
            keys, values = kv_ref[0, window, :], kv_ref[1, window, :]
            column = lax.broadcasted_iota(jnp.int32, (rows, size), 1)
            seen = column >= low
            last = lax.broadcasted_iota(jnp.int32, (rows, rows), 1) <= row
            found = []
            for h in range(heads):
                cut = slice(h * HEAD, (h + 1) * HEAD)
                scores = scores_of(q_ref[at, cut], keys)
                tail = jnp.where(last, scores[:, before * rows :], FILL)
                if before:
                    tail = jnp.concatenate([scores[:, : before * rows], tail], axis=1)
                scores = jnp.where(seen, tail, FILL)
                top = jnp.max(scores, axis=1, keepdims=True)
                weights = decay(scores, top)
                found += [top, jnp.sum(weights, axis=1, keepdims=True)]
                acc_s[:, cut] = jnp.dot(
                    weights.astype(jnp.bfloat16), values, preferred_element_type=jnp.float32
                )
            stat_s[...] = pack(found)

        for before in range(longest + 1):
            pl.when(count == before)(lambda before=before: fold(before))

        @pl.when(slot < early)
        def _():
            here = span(slot, rows)
            for h in range(heads):
                _, total, acc = joined(
                    part_of(acc_s, stat_s, slice(None), h), part_of(acc_pre, stat_pre, here, h)
                )
                done_ref[here, h * HEAD : (h + 1) * HEAD] = (acc / total).astype(done_ref.dtype)

        @pl.when(slot >= early)
        def _():
            here = span(slot - early, rows)
            acc_ref[here, :] = acc_s[...]
            stat_ref[here, :] = stat_s[...]

        return c

    lax.fori_loop(0, positions // rows, do, 0)


def attend_new(docs, queries, kv, acc, stat, rows):
    positions, width = queries.shape
    early = acc.shape[0] // rows
    late = positions - rows * early
    smem = pl.BlockSpec(memory_space=pltpu.SMEM)
    vmem = pl.BlockSpec(memory_space=pltpu.VMEM)
    return pl.pallas_call(
        lambda *refs: new_kernel(early, *refs),
        out_shape=(
            jax.ShapeDtypeStruct((rows * early, width), queries.dtype),
            jax.ShapeDtypeStruct((late, width), jnp.float32),
            jax.ShapeDtypeStruct((late, HEAD), jnp.float32),
        ),
        in_specs=[smem, vmem, vmem, vmem, vmem],
        out_specs=(vmem, vmem, vmem),
        scratch_shapes=[
            pltpu.VMEM((rows, width), jnp.float32),
            pltpu.VMEM((rows, HEAD), jnp.float32),
            pltpu.SMEM((docs.shape[1],), jnp.int32),
        ],
        compiler_params=pltpu.CompilerParams(vmem_limit_bytes=40 << 20),
        name="attend_new",
    )(docs, queries, kv, acc, stat)


def finish_kernel(
    columns, early, pages, q_ref, pre_ref, done_ref, acc_ref, stat_ref, out_ref, stage, send, recv, near
):
    me = lax.axis_index("ctx")
    positions, width = q_ref.shape
    rows = positions // columns
    heads = width // HEAD
    live = pages[0] * (pre_ref.shape[1] // 64)

    barrier = pltpu.get_barrier_semaphore()

    def greet(r):
        to = partner(me, r, columns, False)
        pl.semaphore_signal(barrier, inc=1, device_id={"ctx": to}, device_id_type=MESH)

    each(1, columns, greet)
    pl.semaphore_wait(barrier, columns - 1)

    def cut_of(device):
        return out_ref.at[:, span(device, width)]

    def send_block(source, r):
        to = partner(me, r, columns, False)
        return pltpu.make_async_remote_copy(
            source, cut_of(me), send.at[r], recv.at[me], device_id={"ctx": to}, device_id_type=MESH
        )

    def send_early(r):
        send_block(done_ref.at[span(r, rows), :], r).start()

    each(1, early, send_early)
    mine = pltpu.make_async_copy(done_ref.at[0:rows, :], cut_of(me), near)
    mine.start()

    def late(i):
        at = span(partner(me, early + i, columns, False), rows)
        here = span(i, rows)
        for h in range(heads):
            cut = slice(h * HEAD, (h + 1) * HEAD)
            _, total, acc = joined(
                part_of(acc_ref, stat_ref, here, h), prefix_part(q_ref[at, cut], pre_ref, live)
            )
            stage[here, cut] = (acc / total).astype(stage.dtype)
        send_block(stage.at[here, :], early + i).start()

    each(0, columns - early, late)

    def settle(r):
        source = partner(me, r, columns, True)
        pltpu.make_async_remote_copy(
            done_ref.at[0:rows, :], cut_of(source), send.at[0], recv.at[source],
            device_id={"ctx": source}, device_id_type=MESH,
        ).wait_recv()
        send_block(done_ref.at[0:rows, :], r).wait_send()

    each(1, columns, settle)
    mine.wait()


def finish(pages, queries, pre, done, acc, stat, columns):
    positions, width = queries.shape
    rows = positions // columns
    early = done.shape[0] // rows
    vmem = pl.BlockSpec(memory_space=pltpu.VMEM)
    return pl.pallas_call(
        lambda *refs: finish_kernel(columns, early, *refs),
        out_shape=jax.ShapeDtypeStruct((rows, width * columns), queries.dtype),
        in_specs=[pl.BlockSpec(memory_space=pltpu.SMEM), vmem, vmem, vmem, vmem, vmem],
        out_specs=pl.BlockSpec(memory_space=pl.ANY),
        scratch_shapes=[
            pltpu.VMEM((positions - rows * early, width), queries.dtype),
            pltpu.SemaphoreType.DMA((columns,)),
            pltpu.SemaphoreType.DMA((columns,)),
            pltpu.SemaphoreType.DMA,
        ],
        compiler_params=pltpu.CompilerParams(
            collective_id=1, has_side_effects=True, vmem_limit_bytes=40 << 20
        ),
        name="finish",
    )(pages, queries, pre, done, acc, stat)


def local(queries, kv_new, kv_pool, prefix_pages, reader_owner, send_page, tile_doc):
    columns, groups = lax.axis_size("ctx"), lax.axis_size("req")
    rows = queries.shape[1]
    q, kv, pre, acc, stat = gather(
        send_page, reader_owner, prefix_pages, kv_pool, queries[0], kv_new[0], columns, groups, EARLY
    )
    done, acc, stat = attend_new(tile_doc, q, kv, acc, stat, rows)
    pre = pre.reshape(2, -1, HEAD)
    return finish(prefix_pages, q, pre, done, acc, stat, columns)[None]


def solution(mesh):
    in_specs = (
        P("req", "ctx", None),
        P("req", None, "ctx", None),
        P(("req", "ctx"), None, None, None),
        P("req"),
        P("req", "ctx", None),
        P("req", "ctx", None),
        P("req", None),
    )
    return jax.shard_map(
        local, mesh=mesh, in_specs=in_specs, out_specs=P("req", "ctx", None), check_vma=False
    )
```

```python
import functools
import math

import jax
import jax.numpy as jnp
from jax import lax
from jax.experimental import pallas as pl
from jax.experimental.pallas import tpu as pltpu
from jax.sharding import PartitionSpec as P

HEAD = 128
TILE = 128
LONGEST = 16
CHUNK = 512
FILL = -1e30
SCALE = math.log2(math.e) / math.sqrt(HEAD)
MESH = pl.DeviceIdType.MESH
EARLY = 11
FIRST = 4


def scores_of(queries, keys):
    return lax.dot_general(
        queries, keys, (((1,), (1,)), ((), ())), preferred_element_type=jnp.float32
    )


def decay(scores, top):
    return jnp.exp2((scores - top) * SCALE)


def attention(units, chunks):
    def score(unit, chunk):
        scores = scores_of(unit(), chunk[0]())
        return scores if chunk[2] is None else jnp.where(chunk[2](), scores, FILL)

    found = []
    ahead = [score(units[0], chunk) for chunk in chunks]
    for at in range(len(units)):
        scores, ahead = ahead, []
        top = functools.reduce(
            jnp.maximum, [jnp.max(s, axis=1, keepdims=True) for s in scores]
        )
        total = acc = 0.0
        for s, chunk in zip(scores, chunks):
            if at + 1 < len(units):
                ahead.append(score(units[at + 1], chunk))
            weights = decay(s, top)
            total = total + jnp.sum(weights, axis=1, keepdims=True)
            acc = acc + jnp.dot(
                weights.astype(jnp.bfloat16), chunk[1](), preferred_element_type=jnp.float32
            )
        found.append((top, total, acc))
    return found


def units_of(q_ref, at, heads):
    return [lambda h=h: q_ref[at, h * HEAD : (h + 1) * HEAD] for h in range(heads)]


def cuts(size):
    return [(start, min(CHUNK, size - start)) for start in range(0, size, CHUNK)]


def prefix_chunks(pre_ref, rows, live):
    keys = pre_ref.shape[1]

    def chunk(start, size):
        def seen():
            return lax.broadcasted_iota(jnp.int32, (rows, size), 1) < live - start

        return (
            lambda: pre_ref[0, start : start + size, :],
            lambda: pre_ref[1, start : start + size, :],
            seen if start + size > keys // 2 else None,
        )

    return [chunk(*cut) for cut in cuts(keys)]


def new_chunk(kv_ref, start, size, seen):
    window = pl.ds(pl.multiple_of(start, HEAD), size)
    return (lambda: kv_ref[0, window, :], lambda: kv_ref[1, window, :], seen)


def document_starts(docs, starts):
    starts[0] = 0

    def begin_of(t):
        starts[t] = jnp.where(docs[0, t] == docs[0, t - 1], starts[t - 1], t)

    each(1, docs.shape[1], begin_of)


def first_seen(starts, block, rows):
    per = rows // TILE
    row = lax.broadcasted_iota(jnp.int32, (rows, 1), 0)
    low = jnp.full((rows, 1), starts[block * per] * TILE, jnp.int32)
    for t in range(1, per):
        low = jnp.where(row >= t * TILE, starts[block * per + t] * TILE, low)
    return row, low


def joined(one, two):
    top = jnp.maximum(one[0], two[0])
    left, right = decay(one[0], top), decay(two[0], top)
    return top, one[1] * left + two[1] * right, one[2] * left + two[2] * right


def pack(tops_and_totals):
    shape = (tops_and_totals[0].shape[0], HEAD)
    lane = lax.broadcasted_iota(jnp.int32, shape, 1)
    stat = jnp.zeros(shape, jnp.float32)
    for at, column in enumerate(tops_and_totals):
        stat = jnp.where(lane == at, column, stat)
    return stat


def part_of(acc_ref, stat_ref, at, h):
    return (
        stat_ref[at, 2 * h : 2 * h + 1],
        stat_ref[at, 2 * h + 1 : 2 * h + 2],
        acc_ref[at, h * HEAD : (h + 1) * HEAD],
    )


def span(index, size):
    start = index * size
    return pl.ds(start if isinstance(start, int) else pl.multiple_of(start, size), size)


def partner(me, r, columns, sends):
    chips_x = columns // 4
    x, z, core = me // 4, (me // 2) % 2, me % 2
    x = (x + r // 4) % chips_x if sends else (x + chips_x - r // 4) % chips_x
    return x * 4 + ((z + r) % 2) * 2 + (core + r // 2) % 2


def partner_chip(chip, t, chips, sends):
    chips_x = chips // 2
    x, z = chip // 2, chip % 2
    x = (x + t // 2) % chips_x if sends else (x + chips_x - t // 2) % chips_x
    return x * 2 + (z + t) % 2


def each(first, last, act):
    def step(t, c):
        act(t)
        return c

    lax.fori_loop(first, last, step, 0)


def gather_kernel(
    columns, groups, early, wanted_ref, owners_ref, pages, pool_ref, q_ref, new_ref,
    q_all, kv_all, pre_all, acc_ref, stat_ref,
    wanted, owners, pool, outgoing, arrived, staged, req_send, req_recv, q_send, q_recv, kv_send, kv_recv,
    kv_pass, pre_send, pre_recv, pre_pass, near,
):
    me = lax.axis_index("ctx")
    group = lax.axis_index("req")
    chips = columns // 2
    chip = me // 2
    core = me % 2
    sibling = chip * 2 + (1 - core)
    rows = q_ref.shape[0]
    width = q_all.shape[1]
    heads = width // HEAD
    slots, page_len = staged.shape[1], staged.shape[2]
    first = FIRST
    loads = [
        pltpu.make_async_copy(source, here, near.at[3 + i])
        for i, (source, here) in enumerate(
            ((pool_ref, pool), (wanted_ref, wanted), (owners_ref, owners))
        )
    ]
    for load in loads:
        load.start()

    barrier = pltpu.get_barrier_semaphore()

    def greet_column(r):
        to = partner(me, r, columns, True)
        pl.semaphore_signal(barrier, inc=1, device_id={"ctx": to}, device_id_type=MESH)

    def greet_group(t):
        to = (group + t) % groups
        pl.semaphore_signal(barrier, inc=1, device_id={"req": to}, device_id_type=MESH)

    each(1, groups, greet_group)
    each(1, columns, greet_column)
    for load in loads:
        load.wait()
    for g in range(groups):
        outgoing[g] = pool[jnp.maximum(wanted[0, 0, g], 0)]
    arrived[group] = outgoing[group]
    pl.semaphore_wait(barrier, columns + groups - 2)

    def page_copy(t):
        to = (group + t) % groups
        return pltpu.make_async_remote_copy(
            outgoing.at[to], arrived.at[group], req_send.at[t], req_recv.at[group],
            device_id={"req": to}, device_id_type=MESH,
        )

    def q_cut(device):
        return q_ref.at[:, span(device, width)]

    def q_slot(device):
        return q_all.at[span(device, rows), :]

    def kv_slot(device):
        return kv_all.at[:, span(device, rows), :]

    def pre_slot(device):
        return pre_all.at[:, :, device]

    def new_cut(at):
        return new_ref.at[:, :, span(at, HEAD)]

    def pre_cut(at):
        return staged.at[:, :, :, span(at, HEAD)]

    def q_copy(r):
        to = partner(me, r, columns, True)
        return pltpu.make_async_remote_copy(
            q_cut(to), q_slot(me), q_send.at[r], q_recv.at[me],
            device_id={"ctx": to}, device_id_type=MESH,
        )

    def kv_copy(t):
        to = partner_chip(chip, t, chips, True)
        return pltpu.make_async_remote_copy(
            new_cut(to), kv_slot(me), kv_send.at[t], kv_recv.at[me],
            device_id={"ctx": to * 2 + core}, device_id_type=MESH,
        )

    def pre_copy(t):
        to = partner_chip(chip, t, chips, True)
        return pltpu.make_async_remote_copy(
            pre_cut(to), pre_slot(me), pre_send.at[t], pre_recv.at[me],
            device_id={"ctx": to * 2 + core}, device_id_type=MESH,
        )

    def source_of(t):
        return partner_chip(chip, t, chips, False) * 2 + core

    def to_sibling(source_ref, slot, send, recv):
        return pltpu.make_async_remote_copy(
            source_ref, slot, send, recv, device_id={"ctx": sibling}, device_id_type=MESH
        )

    def kv_onward(t):
        slot = kv_slot(source_of(t))
        return to_sibling(slot, slot, kv_pass.at[t], kv_recv.at[source_of(t)])

    def pre_onward(t):
        slot = pre_slot(source_of(t))
        return to_sibling(slot, slot, pre_pass.at[t], pre_recv.at[source_of(t)])

    kv_twin = to_sibling(new_cut(chip), kv_slot(me), kv_pass.at[0], kv_recv.at[me])
    pre_twin = to_sibling(pre_cut(chip), pre_slot(me), pre_pass.at[0], pre_recv.at[me])
    own = [
        pltpu.make_async_copy(q_cut(me), q_slot(me), near.at[0]),
        pltpu.make_async_copy(new_cut(chip), kv_slot(me), near.at[1]),
        pltpu.make_async_copy(pre_cut(chip), pre_slot(me), near.at[2]),
    ]

    each(1, groups, lambda t: page_copy(t).start())
    each(1, first, lambda r: q_copy(r).start())
    own[0].start()
    own[1].start()

    def page_arrival(t):
        source = (group + groups - t) % groups
        pltpu.make_async_remote_copy(
            outgoing.at[source], arrived.at[source], req_send.at[0], req_recv.at[source],
            device_id={"req": source}, device_id_type=MESH,
        ).wait_recv()

    each(1, groups, page_arrival)
    for i in range(slots):
        staged[:, i] = arrived[jnp.maximum(owners[0, 0, i], 0)]
    each(1, chips, lambda t: pre_copy(t).start())
    pre_twin.start()
    own[2].start()
    each(first, columns, lambda r: q_copy(r).start())
    each(1, chips, lambda t: kv_copy(t).start())
    kv_twin.start()

    def pre_relay(t):
        pre_onward(t).wait_recv()
        pre_onward(t).start()

    each(1, chips, pre_relay)

    def pre_twin_arrival(t):
        source = partner_chip(chip, t, chips, False) * 2 + (1 - core)
        to_sibling(pre_slot(source), pre_slot(source), near.at[3], pre_recv.at[source]).wait_recv()

    each(0, chips, pre_twin_arrival)
    own[0].wait()
    own[2].wait()
    keys = slots * columns * page_len
    live = pages[0] * page_len
    prefix = pre_all.reshape(2, keys, HEAD)

    def q_arrival(r):
        source = partner(me, r, columns, False)
        pltpu.make_async_remote_copy(
            q_slot(source), q_slot(source), q_send.at[0], q_recv.at[source],
            device_id={"ctx": source}, device_id_type=MESH,
        ).wait_recv()

    def attend(r):
        at = span(partner(me, r, columns, False), rows)
        out = span(r, rows)
        parts = attention(units_of(q_all, at, heads), prefix_chunks(prefix, rows, live))
        for h, part in enumerate(parts):
            acc_ref[out, h * HEAD : (h + 1) * HEAD] = part[2]
        stat_ref[out, :] = pack([column for part in parts for column in part[:2]])

    attend(0)

    def arrive_and_attend(r):
        q_arrival(r)
        attend(r)

    each(1, early, arrive_and_attend)

    def kv_relay(t):
        kv_onward(t).wait_recv()
        kv_onward(t).start()

    each(1, chips, kv_relay)
    each(early, columns, q_arrival)

    def kv_twin_arrival(t):
        source = partner_chip(chip, t, chips, False) * 2 + (1 - core)
        to_sibling(kv_slot(source), kv_slot(source), near.at[3], kv_recv.at[source]).wait_recv()

    each(0, chips, kv_twin_arrival)
    each(1, groups, lambda t: page_copy(t).wait_send())
    each(1, columns, lambda r: q_copy(r).wait_send())
    for copies in (kv_copy, pre_copy, kv_onward, pre_onward):
        each(1, chips, lambda t, copies=copies: copies(t).wait_send())
    kv_twin.wait_send()
    pre_twin.wait_send()
    own[1].wait()


def in_hbm(x):
    return pltpu.with_memory_space_constraint(x, pltpu.HBM)


def gather(wanted, owners, pages, pool, queries, kv_new, columns, groups, early):
    rows, features = queries.shape
    slots, page_len = owners.shape[2], pool.shape[2]
    dtype = queries.dtype
    width = features // columns
    dma = pltpu.SemaphoreType.DMA
    smem = pl.BlockSpec(memory_space=pltpu.SMEM)
    vmem = pl.BlockSpec(memory_space=pltpu.VMEM)
    hbm = pl.BlockSpec(memory_space=pltpu.HBM)
    chips = columns // 2
    return pl.pallas_call(
        lambda *refs: gather_kernel(columns, groups, early, *refs),
        out_shape=(
            jax.ShapeDtypeStruct((rows * columns, width), dtype),
            jax.ShapeDtypeStruct((2, rows * columns, HEAD), dtype),
            jax.ShapeDtypeStruct((2, slots, columns, page_len, HEAD), dtype),
            jax.ShapeDtypeStruct((rows * early, width), jnp.float32),
            jax.ShapeDtypeStruct((rows * early, HEAD), jnp.float32),
        ),
        in_specs=[hbm, hbm, smem, hbm, hbm, hbm],
        out_specs=(vmem, vmem, vmem, vmem, vmem),
        scratch_shapes=[
            pltpu.SMEM(wanted.shape, jnp.int32),
            pltpu.SMEM(owners.shape, jnp.int32),
            pltpu.VMEM(pool.shape, dtype),
            pltpu.VMEM((groups,) + pool.shape[1:], dtype),
            pltpu.VMEM((groups,) + pool.shape[1:], dtype),
            pltpu.VMEM((2, slots) + pool.shape[2:], dtype),
            dma((groups,)), dma((groups,)),
            dma((columns,)), dma((columns,)),
            dma((chips,)), dma((columns,)), dma((chips,)),
            dma((chips,)), dma((columns,)), dma((chips,)),
            dma((6,)),
        ],
        compiler_params=pltpu.CompilerParams(
            collective_id=0, has_side_effects=True, vmem_limit_bytes=32 << 20
        ),
        name="gather",
    )(
        in_hbm(wanted), in_hbm(owners), pages, in_hbm(pool), in_hbm(queries), in_hbm(kv_new)
    )


def new_kernel(columns, docs, q_ref, kv_ref, acc_pre, stat_pre, done_ref, acc_s, stat_s, starts):
    me = lax.axis_index("ctx")
    rows, width = acc_s.shape
    heads = width // HEAD
    per = rows // TILE
    document_starts(docs, starts)

    def do(slot):
        block = partner(me, slot, columns, False)
        begin = starts[block * per] // per
        row, low = first_seen(starts, block, rows)
        at = span(block, rows)

        def fold(before):
            def seen(start, size):
                return lax.broadcasted_iota(jnp.int32, (rows, size), 1) + start >= low

            def chunk(offset, size):
                start = begin * rows + offset
                return new_chunk(kv_ref, start, size, lambda: seen(start, size))

            def last():
                column = lax.broadcasted_iota(jnp.int32, (rows, rows), 1)
                return seen(block * rows, rows) & (column <= row)

            chunks = [chunk(*cut) for cut in cuts(before * rows)]
            chunks.append(new_chunk(kv_ref, block * rows, rows, last))
            parts = attention(units_of(q_ref, at, heads), chunks)
            for h, part in enumerate(parts):
                acc_s[:, h * HEAD : (h + 1) * HEAD] = part[2]
            stat_s[...] = pack([column for part in parts for column in part[:2]])

        for before in range(LONGEST // per + 1):
            pl.when(block - begin == before)(lambda before=before: fold(before))

        here = span(slot, rows)
        for h in range(heads):
            _, total, acc = joined(
                part_of(acc_s, stat_s, slice(None), h), part_of(acc_pre, stat_pre, here, h)
            )
            done_ref[here, h * HEAD : (h + 1) * HEAD] = (acc / total).astype(done_ref.dtype)

    each(0, done_ref.shape[0] // rows, do)


def attend_new(docs, queries, kv, acc, stat, rows):
    positions, width = queries.shape
    smem = pl.BlockSpec(memory_space=pltpu.SMEM)
    vmem = pl.BlockSpec(memory_space=pltpu.VMEM)
    return pl.pallas_call(
        lambda *refs: new_kernel(positions // rows, *refs),
        out_shape=jax.ShapeDtypeStruct(acc.shape, queries.dtype),
        in_specs=[smem, vmem, vmem, vmem, vmem],
        out_specs=vmem,
        scratch_shapes=[
            pltpu.VMEM((rows, width), jnp.float32),
            pltpu.VMEM((rows, HEAD), jnp.float32),
            pltpu.SMEM((docs.shape[1],), jnp.int32),
        ],
        compiler_params=pltpu.CompilerParams(vmem_limit_bytes=40 << 20),
        name="attend_new",
    )(docs, queries, kv, acc, stat)


def finish_kernel(
    columns, pages, docs, q_ref, pre_ref, kv_ref, done_ref, out_ref, stage, starts, send, recv, near
):
    me = lax.axis_index("ctx")
    positions, width = q_ref.shape
    rows = positions // columns
    heads = width // HEAD
    early = done_ref.shape[0] // rows
    live = pages[0] * (pre_ref.shape[1] // 64)

    barrier = pltpu.get_barrier_semaphore()

    def greet(r):
        to = partner(me, r, columns, False)
        pl.semaphore_signal(barrier, inc=1, device_id={"ctx": to}, device_id_type=MESH)

    each(1, columns, greet)
    document_starts(docs, starts)
    pl.semaphore_wait(barrier, columns - 1)

    def cut_of(device):
        return out_ref.at[:, span(device, width)]

    def send_block(source, r):
        to = partner(me, r, columns, False)
        return pltpu.make_async_remote_copy(
            source, cut_of(me), send.at[r], recv.at[me], device_id={"ctx": to}, device_id_type=MESH
        )

    each(1, early, lambda r: send_block(done_ref.at[span(r, rows), :], r).start())
    mine = pltpu.make_async_copy(done_ref.at[0:rows, :], cut_of(me), near)
    mine.start()
    longest = LONGEST * TILE // rows

    def late(i):
        block = partner(me, early + i, columns, False)
        row, low = first_seen(starts, block, rows)
        begin = jnp.maximum(block - longest, 0) * rows

        def chunk(offset, size):
            start = begin + offset

            def seen():
                column = lax.broadcasted_iota(jnp.int32, (rows, size), 1) + start
                return (column >= low) & (column <= row + block * rows)

            return new_chunk(kv_ref, start, size, seen)

        chunks = prefix_chunks(pre_ref, rows, live)
        chunks += [chunk(*cut) for cut in cuts((longest + 1) * rows)]
        here = span(i, rows)
        for h, part in enumerate(attention(units_of(q_ref, span(block, rows), heads), chunks)):
            stage[here, h * HEAD : (h + 1) * HEAD] = (part[2] / part[1]).astype(stage.dtype)
        send_block(stage.at[here, :], early + i).start()

    each(0, columns - early, late)

    def settle(r):
        source = partner(me, r, columns, True)
        pltpu.make_async_remote_copy(
            done_ref.at[0:rows, :], cut_of(source), send.at[0], recv.at[source],
            device_id={"ctx": source}, device_id_type=MESH,
        ).wait_recv()
        send_block(done_ref.at[0:rows, :], r).wait_send()

    each(1, columns, settle)
    mine.wait()


def finish(pages, docs, queries, pre, kv, done, columns):
    positions, width = queries.shape
    smem = pl.BlockSpec(memory_space=pltpu.SMEM)
    vmem = pl.BlockSpec(memory_space=pltpu.VMEM)
    return pl.pallas_call(
        lambda *refs: finish_kernel(columns, *refs),
        out_shape=jax.ShapeDtypeStruct((positions // columns, width * columns), queries.dtype),
        in_specs=[smem, smem, vmem, vmem, vmem, vmem],
        out_specs=pl.BlockSpec(memory_space=pl.ANY),
        scratch_shapes=[
            pltpu.VMEM((positions - done.shape[0], width), queries.dtype),
            pltpu.SMEM((docs.shape[1],), jnp.int32),
            pltpu.SemaphoreType.DMA((columns,)),
            pltpu.SemaphoreType.DMA((columns,)),
            pltpu.SemaphoreType.DMA,
        ],
        compiler_params=pltpu.CompilerParams(
            collective_id=1, has_side_effects=True, vmem_limit_bytes=40 << 20
        ),
        name="finish",
    )(pages, docs, queries, pre, kv, done)


def local(queries, kv_new, kv_pool, prefix_pages, reader_owner, send_page, tile_doc):
    columns, groups = lax.axis_size("ctx"), lax.axis_size("req")
    q, kv, pre, acc, stat = gather(
        send_page, reader_owner, prefix_pages, kv_pool, queries[0], kv_new[0], columns, groups, EARLY
    )
    done = attend_new(tile_doc, q, kv, acc, stat, queries.shape[1])
    return finish(prefix_pages, tile_doc, q, pre.reshape(2, -1, HEAD), kv, done, columns)[None]


def solution(mesh):
    in_specs = (
        P("req", "ctx", None),
        P("req", None, "ctx", None),
        P(("req", "ctx"), None, None, None),
        P("req"),
        P("req", "ctx", None),
        P("req", "ctx", None),
        P("req", None),
    )
    return jax.shard_map(
        local, mesh=mesh, in_specs=in_specs, out_specs=P("req", "ctx", None), check_vma=False
    )
```

```python
import functools
import math

import jax
import jax.numpy as jnp
from jax import lax
from jax.experimental import pallas as pl
from jax.experimental.pallas import tpu as pltpu
from jax.sharding import PartitionSpec as P

HEAD = 128
TILE = 128
LONGEST = 16
CHUNK = 512
FILL = -1e30
SCALE = math.log2(math.e) / math.sqrt(HEAD)
MESH = pl.DeviceIdType.MESH
EARLY = 11
FIRST = 4


def scores_of(queries, keys):
    return lax.dot_general(
        queries, keys, (((1,), (1,)), ((), ())), preferred_element_type=jnp.float32
    )


def decay(scores, top):
    return jnp.exp2((scores - top) * SCALE)


def attention(units, chunks):
    def score(unit, chunk):
        scores = scores_of(unit(), chunk[0]())
        return scores if chunk[2] is None else jnp.where(chunk[2](), scores, FILL)

    found = []
    ahead = [score(units[0], chunk) for chunk in chunks]
    for at in range(len(units)):
        scores, ahead = ahead, []
        top = functools.reduce(
            jnp.maximum, [jnp.max(s, axis=1, keepdims=True) for s in scores]
        )
        total = acc = 0.0
        for s, chunk in zip(scores, chunks):
            if at + 1 < len(units):
                ahead.append(score(units[at + 1], chunk))
            weights = decay(s, top)
            total = total + jnp.sum(weights, axis=1, keepdims=True)
            acc = acc + jnp.dot(
                weights.astype(jnp.bfloat16), chunk[1](), preferred_element_type=jnp.float32
            )
        found.append((top, total, acc))
    return found


def units_of(q_ref, at, heads):
    return [lambda h=h: q_ref[at, h * HEAD : (h + 1) * HEAD] for h in range(heads)]


def cuts(size):
    return [(start, min(CHUNK, size - start)) for start in range(0, size, CHUNK)]


def prefix_chunks(pre_ref, rows, live):
    keys = pre_ref.shape[1]

    def chunk(start, size):
        def seen():
            return lax.broadcasted_iota(jnp.int32, (rows, size), 1) < live - start

        return (
            lambda: pre_ref[0, start : start + size, :],
            lambda: pre_ref[1, start : start + size, :],
            seen if start + size > keys // 2 else None,
        )

    return [chunk(*cut) for cut in cuts(keys)]


def new_chunk(kv_ref, start, size, seen):
    window = pl.ds(pl.multiple_of(start, HEAD), size)
    return (lambda: kv_ref[0, window, :], lambda: kv_ref[1, window, :], seen)


def document_starts(docs, starts):
    starts[0] = 0

    def begin_of(t):
        starts[t] = jnp.where(docs[0, t] == docs[0, t - 1], starts[t - 1], t)

    each(1, docs.shape[1], begin_of)


def seen_by(starts, block, rows, start, size, causal):
    per = rows // TILE
    tiles = []
    for t in range(per):
        tile = block * per + t
        column = lax.broadcasted_iota(jnp.int32, (TILE, size), 1)
        seen = column >= starts[tile] * TILE - start
        if causal:
            row = lax.broadcasted_iota(jnp.int32, (TILE, size), 0)
            seen = seen & (column - row <= tile * TILE - start)
        tiles.append(seen)
    return jnp.concatenate(tiles, axis=0)


def joined(one, two):
    top = jnp.maximum(one[0], two[0])
    left, right = decay(one[0], top), decay(two[0], top)
    return top, one[1] * left + two[1] * right, one[2] * left + two[2] * right


def pack(columns):
    return jnp.concatenate(
        [jnp.broadcast_to(column, (column.shape[0], HEAD)) for column in columns], axis=1
    )


def part_of(acc_ref, stat_ref, at, h):
    return (
        stat_ref[at, 2 * h * HEAD : (2 * h + 1) * HEAD],
        stat_ref[at, (2 * h + 1) * HEAD : (2 * h + 2) * HEAD],
        acc_ref[at, h * HEAD : (h + 1) * HEAD],
    )


def span(index, size):
    start = index * size
    return pl.ds(start if isinstance(start, int) else pl.multiple_of(start, size), size)


def partner(me, r, columns, sends):
    chips_x = columns // 4
    x, z, core = me // 4, (me // 2) % 2, me % 2
    x = (x + r // 4) % chips_x if sends else (x + chips_x - r // 4) % chips_x
    return x * 4 + ((z + r) % 2) * 2 + (core + r // 2) % 2


def partner_chip(chip, t, chips, sends):
    chips_x = chips // 2
    x, z = chip // 2, chip % 2
    x = (x + t // 2) % chips_x if sends else (x + chips_x - t // 2) % chips_x
    return x * 2 + (z + t) % 2


def each(first, last, act):
    def step(t, c):
        act(t)
        return c

    lax.fori_loop(first, last, step, 0)


def gather_kernel(
    columns, groups, early, wanted_ref, owners_ref, pages, pool_ref, q_ref, new_ref,
    q_all, kv_all, pre_all, acc_ref, stat_ref,
    wanted, owners, pool, outgoing, arrived, staged, req_send, req_recv, q_send, q_recv, kv_send, kv_recv,
    kv_pass, pre_send, pre_recv, pre_pass, near,
):
    me = lax.axis_index("ctx")
    group = lax.axis_index("req")
    chips = columns // 2
    chip = me // 2
    core = me % 2
    sibling = chip * 2 + (1 - core)
    rows = q_ref.shape[0]
    width = q_all.shape[1]
    heads = width // HEAD
    slots, page_len = staged.shape[1], staged.shape[2]
    first = FIRST
    loads = [
        pltpu.make_async_copy(source, here, near.at[3 + i])
        for i, (source, here) in enumerate(
            ((pool_ref, pool), (wanted_ref, wanted), (owners_ref, owners))
        )
    ]
    for load in loads:
        load.start()

    barrier = pltpu.get_barrier_semaphore()

    def greet_column(r):
        to = partner(me, r, columns, True)
        pl.semaphore_signal(barrier, inc=1, device_id={"ctx": to}, device_id_type=MESH)

    def greet_group(t):
        to = (group + t) % groups
        pl.semaphore_signal(barrier, inc=1, device_id={"req": to}, device_id_type=MESH)

    each(1, groups, greet_group)
    each(1, columns, greet_column)
    for load in loads:
        load.wait()
    for g in range(groups):
        outgoing[g] = pool[jnp.maximum(wanted[0, 0, g], 0)]
    arrived[group] = outgoing[group]
    pl.semaphore_wait(barrier, columns + groups - 2)

    def page_copy(t):
        to = (group + t) % groups
        return pltpu.make_async_remote_copy(
            outgoing.at[to], arrived.at[group], req_send.at[t], req_recv.at[group],
            device_id={"req": to}, device_id_type=MESH,
        )

    def q_cut(device):
        return q_ref.at[:, span(device, width)]

    def q_slot(device):
        return q_all.at[span(device, rows), :]

    def kv_slot(device):
        return kv_all.at[:, span(device, rows), :]

    def pre_slot(device):
        return pre_all.at[:, :, device]

    def new_cut(at):
        return new_ref.at[:, :, span(at, HEAD)]

    def pre_cut(at):
        return staged.at[:, :, :, span(at, HEAD)]

    def q_copy(r):
        to = partner(me, r, columns, True)
        return pltpu.make_async_remote_copy(
            q_cut(to), q_slot(me), q_send.at[r], q_recv.at[me],
            device_id={"ctx": to}, device_id_type=MESH,
        )

    def kv_copy(t):
        to = partner_chip(chip, t, chips, True)
        return pltpu.make_async_remote_copy(
            new_cut(to), kv_slot(me), kv_send.at[t], kv_recv.at[me],
            device_id={"ctx": to * 2 + core}, device_id_type=MESH,
        )

    def pre_copy(t):
        to = partner_chip(chip, t, chips, True)
        return pltpu.make_async_remote_copy(
            pre_cut(to), pre_slot(me), pre_send.at[t], pre_recv.at[me],
            device_id={"ctx": to * 2 + core}, device_id_type=MESH,
        )

    def source_of(t):
        return partner_chip(chip, t, chips, False) * 2 + core

    def to_sibling(source_ref, slot, send, recv):
        return pltpu.make_async_remote_copy(
            source_ref, slot, send, recv, device_id={"ctx": sibling}, device_id_type=MESH
        )

    def kv_onward(t):
        slot = kv_slot(source_of(t))
        return to_sibling(slot, slot, kv_pass.at[t], kv_recv.at[source_of(t)])

    def pre_onward(t):
        slot = pre_slot(source_of(t))
        return to_sibling(slot, slot, pre_pass.at[t], pre_recv.at[source_of(t)])

    kv_twin = to_sibling(new_cut(chip), kv_slot(me), kv_pass.at[0], kv_recv.at[me])
    pre_twin = to_sibling(pre_cut(chip), pre_slot(me), pre_pass.at[0], pre_recv.at[me])
    own = [
        pltpu.make_async_copy(q_cut(me), q_slot(me), near.at[0]),
        pltpu.make_async_copy(new_cut(chip), kv_slot(me), near.at[1]),
        pltpu.make_async_copy(pre_cut(chip), pre_slot(me), near.at[2]),
    ]

    each(1, groups, lambda t: page_copy(t).start())
    each(1, first, lambda r: q_copy(r).start())
    own[0].start()
    own[1].start()

    def page_arrival(t):
        source = (group + groups - t) % groups
        pltpu.make_async_remote_copy(
            outgoing.at[source], arrived.at[source], req_send.at[0], req_recv.at[source],
            device_id={"req": source}, device_id_type=MESH,
        ).wait_recv()

    each(1, groups, page_arrival)
    for i in range(slots):
        staged[:, i] = arrived[jnp.maximum(owners[0, 0, i], 0)]
    each(1, chips, lambda t: pre_copy(t).start())
    pre_twin.start()
    own[2].start()
    each(first, columns, lambda r: q_copy(r).start())
    each(1, chips, lambda t: kv_copy(t).start())
    kv_twin.start()

    def pre_relay(t):
        pre_onward(t).wait_recv()
        pre_onward(t).start()

    each(1, chips, pre_relay)

    def pre_twin_arrival(t):
        source = partner_chip(chip, t, chips, False) * 2 + (1 - core)
        to_sibling(pre_slot(source), pre_slot(source), near.at[3], pre_recv.at[source]).wait_recv()

    each(0, chips, pre_twin_arrival)
    own[0].wait()
    own[2].wait()
    keys = slots * columns * page_len
    live = pages[0] * page_len
    prefix = pre_all.reshape(2, keys, HEAD)

    def q_arrival(r):
        source = partner(me, r, columns, False)
        pltpu.make_async_remote_copy(
            q_slot(source), q_slot(source), q_send.at[0], q_recv.at[source],
            device_id={"ctx": source}, device_id_type=MESH,
        ).wait_recv()

    def attend(r):
        at = span(partner(me, r, columns, False), rows)
        out = span(r, rows)
        parts = attention(units_of(q_all, at, heads), prefix_chunks(prefix, rows, live))
        for h, part in enumerate(parts):
            acc_ref[out, h * HEAD : (h + 1) * HEAD] = part[2]
        stat_ref[out, :] = pack([column for part in parts for column in part[:2]])

    attend(0)

    def arrive_and_attend(r):
        q_arrival(r)
        attend(r)

    each(1, early, arrive_and_attend)

    def kv_relay(t):
        kv_onward(t).wait_recv()
        kv_onward(t).start()

    each(1, chips, kv_relay)
    each(early, columns, q_arrival)

    def kv_twin_arrival(t):
        source = partner_chip(chip, t, chips, False) * 2 + (1 - core)
        to_sibling(kv_slot(source), kv_slot(source), near.at[3], kv_recv.at[source]).wait_recv()

    each(0, chips, kv_twin_arrival)
    each(1, groups, lambda t: page_copy(t).wait_send())
    each(1, columns, lambda r: q_copy(r).wait_send())
    for copies in (kv_copy, pre_copy, kv_onward, pre_onward):
        each(1, chips, lambda t, copies=copies: copies(t).wait_send())
    kv_twin.wait_send()
    pre_twin.wait_send()
    own[1].wait()


def in_hbm(x):
    return pltpu.with_memory_space_constraint(x, pltpu.HBM)


def gather(wanted, owners, pages, pool, queries, kv_new, columns, groups, early):
    rows, features = queries.shape
    slots, page_len = owners.shape[2], pool.shape[2]
    dtype = queries.dtype
    width = features // columns
    dma = pltpu.SemaphoreType.DMA
    smem = pl.BlockSpec(memory_space=pltpu.SMEM)
    vmem = pl.BlockSpec(memory_space=pltpu.VMEM)
    hbm = pl.BlockSpec(memory_space=pltpu.HBM)
    chips = columns // 2
    return pl.pallas_call(
        lambda *refs: gather_kernel(columns, groups, early, *refs),
        out_shape=(
            jax.ShapeDtypeStruct((rows * columns, width), dtype),
            jax.ShapeDtypeStruct((2, rows * columns, HEAD), dtype),
            jax.ShapeDtypeStruct((2, slots, columns, page_len, HEAD), dtype),
            jax.ShapeDtypeStruct((rows * early, width), jnp.float32),
            jax.ShapeDtypeStruct((rows * early, 2 * width), jnp.float32),
        ),
        in_specs=[hbm, hbm, smem, hbm, hbm, hbm],
        out_specs=(vmem, vmem, vmem, vmem, vmem),
        scratch_shapes=[
            pltpu.SMEM(wanted.shape, jnp.int32),
            pltpu.SMEM(owners.shape, jnp.int32),
            pltpu.VMEM(pool.shape, dtype),
            pltpu.VMEM((groups,) + pool.shape[1:], dtype),
            pltpu.VMEM((groups,) + pool.shape[1:], dtype),
            pltpu.VMEM((2, slots) + pool.shape[2:], dtype),
            dma((groups,)), dma((groups,)),
            dma((columns,)), dma((columns,)),
            dma((chips,)), dma((columns,)), dma((chips,)),
            dma((chips,)), dma((columns,)), dma((chips,)),
            dma((6,)),
        ],
        compiler_params=pltpu.CompilerParams(
            collective_id=0, has_side_effects=True, vmem_limit_bytes=32 << 20
        ),
        name="gather",
    )(
        in_hbm(wanted), in_hbm(owners), pages, in_hbm(pool), in_hbm(queries), in_hbm(kv_new)
    )


def new_kernel(columns, docs, q_ref, kv_ref, acc_pre, stat_pre, done_ref, acc_s, stat_s, starts):
    me = lax.axis_index("ctx")
    rows, width = acc_s.shape
    heads = width // HEAD
    per = rows // TILE
    document_starts(docs, starts)

    def do(slot):
        block = partner(me, slot, columns, False)
        begin = starts[block * per] // per
        at = span(block, rows)

        def fold(before):
            def chunk(start, size, causal):
                seen = lambda: seen_by(starts, block, rows, start, size, causal)
                return new_chunk(kv_ref, start, size, seen)

            chunks = [chunk(begin * rows + at, size, False) for at, size in cuts(before * rows)]
            chunks.append(chunk(block * rows, rows, True))
            parts = attention(units_of(q_ref, at, heads), chunks)
            for h, part in enumerate(parts):
                acc_s[:, h * HEAD : (h + 1) * HEAD] = part[2]
            stat_s[...] = pack([column for part in parts for column in part[:2]])

        for before in range(LONGEST // per + 1):
            pl.when(block - begin == before)(lambda before=before: fold(before))

        here = span(slot, rows)
        for h in range(heads):
            _, total, acc = joined(
                part_of(acc_s, stat_s, slice(None), h), part_of(acc_pre, stat_pre, here, h)
            )
            done_ref[here, h * HEAD : (h + 1) * HEAD] = (acc / total).astype(done_ref.dtype)

    each(0, done_ref.shape[0] // rows, do)


def attend_new(docs, queries, kv, acc, stat, rows):
    positions, width = queries.shape
    smem = pl.BlockSpec(memory_space=pltpu.SMEM)
    vmem = pl.BlockSpec(memory_space=pltpu.VMEM)
    return pl.pallas_call(
        lambda *refs: new_kernel(positions // rows, *refs),
        out_shape=jax.ShapeDtypeStruct(acc.shape, queries.dtype),
        in_specs=[smem, vmem, vmem, vmem, vmem],
        out_specs=vmem,
        scratch_shapes=[
            pltpu.VMEM((rows, width), jnp.float32),
            pltpu.VMEM((rows, 2 * width), jnp.float32),
            pltpu.SMEM((docs.shape[1],), jnp.int32),
        ],
        compiler_params=pltpu.CompilerParams(vmem_limit_bytes=40 << 20),
        name="attend_new",
    )(docs, queries, kv, acc, stat)


def finish_kernel(
    columns, pages, docs, q_ref, pre_ref, kv_ref, done_ref, out_ref, stage, starts, send, recv, near
):
    me = lax.axis_index("ctx")
    positions, width = q_ref.shape
    rows = positions // columns
    heads = width // HEAD
    early = done_ref.shape[0] // rows
    live = pages[0] * (pre_ref.shape[1] // 64)

    barrier = pltpu.get_barrier_semaphore()

    def greet(r):
        to = partner(me, r, columns, False)
        pl.semaphore_signal(barrier, inc=1, device_id={"ctx": to}, device_id_type=MESH)

    each(1, columns, greet)
    document_starts(docs, starts)
    pl.semaphore_wait(barrier, columns - 1)

    def cut_of(device):
        return out_ref.at[:, span(device, width)]

    def send_block(source, r):
        to = partner(me, r, columns, False)
        return pltpu.make_async_remote_copy(
            source, cut_of(me), send.at[r], recv.at[me], device_id={"ctx": to}, device_id_type=MESH
        )

    each(1, early, lambda r: send_block(done_ref.at[span(r, rows), :], r).start())
    mine = pltpu.make_async_copy(done_ref.at[0:rows, :], cut_of(me), near)
    mine.start()
    longest = LONGEST * TILE // rows

    def late(i):
        block = partner(me, early + i, columns, False)
        begin = jnp.maximum(block - longest, 0) * rows

        def chunk(offset, size):
            start = begin + offset
            seen = lambda: seen_by(starts, block, rows, start, size, True)
            return new_chunk(kv_ref, start, size, seen)

        chunks = prefix_chunks(pre_ref, rows, live)
        chunks += [chunk(*cut) for cut in cuts((longest + 1) * rows)]
        here = span(i, rows)
        for h, part in enumerate(attention(units_of(q_ref, span(block, rows), heads), chunks)):
            stage[here, h * HEAD : (h + 1) * HEAD] = (part[2] / part[1]).astype(stage.dtype)
        send_block(stage.at[here, :], early + i).start()

    each(0, columns - early, late)

    def settle(r):
        source = partner(me, r, columns, True)
        pltpu.make_async_remote_copy(
            done_ref.at[0:rows, :], cut_of(source), send.at[0], recv.at[source],
            device_id={"ctx": source}, device_id_type=MESH,
        ).wait_recv()
        send_block(done_ref.at[0:rows, :], r).wait_send()

    each(1, columns, settle)
    mine.wait()


def finish(pages, docs, queries, pre, kv, done, columns):
    positions, width = queries.shape
    smem = pl.BlockSpec(memory_space=pltpu.SMEM)
    vmem = pl.BlockSpec(memory_space=pltpu.VMEM)
    return pl.pallas_call(
        lambda *refs: finish_kernel(columns, *refs),
        out_shape=jax.ShapeDtypeStruct((positions // columns, width * columns), queries.dtype),
        in_specs=[smem, smem, vmem, vmem, vmem, vmem],
        out_specs=pl.BlockSpec(memory_space=pl.ANY),
        scratch_shapes=[
            pltpu.VMEM((positions - done.shape[0], width), queries.dtype),
            pltpu.SMEM((docs.shape[1],), jnp.int32),
            pltpu.SemaphoreType.DMA((columns,)),
            pltpu.SemaphoreType.DMA((columns,)),
            pltpu.SemaphoreType.DMA,
        ],
        compiler_params=pltpu.CompilerParams(
            collective_id=1, has_side_effects=True, vmem_limit_bytes=40 << 20
        ),
        name="finish",
    )(pages, docs, queries, pre, kv, done)


def local(queries, kv_new, kv_pool, prefix_pages, reader_owner, send_page, tile_doc):
    columns, groups = lax.axis_size("ctx"), lax.axis_size("req")
    q, kv, pre, acc, stat = gather(
        send_page, reader_owner, prefix_pages, kv_pool, queries[0], kv_new[0], columns, groups, EARLY
    )
    done = attend_new(tile_doc, q, kv, acc, stat, queries.shape[1])
    return finish(prefix_pages, tile_doc, q, pre.reshape(2, -1, HEAD), kv, done, columns)[None]


def solution(mesh):
    in_specs = (
        P("req", "ctx", None),
        P("req", None, "ctx", None),
        P(("req", "ctx"), None, None, None),
        P("req"),
        P("req", "ctx", None),
        P("req", "ctx", None),
        P("req", None),
    )
    return jax.shard_map(
        local, mesh=mesh, in_specs=in_specs, out_specs=P("req", "ctx", None), check_vma=False
    )
```

```python
import functools
import math

import jax
import jax.numpy as jnp
from jax import lax
from jax.experimental import pallas as pl
from jax.experimental.pallas import tpu as pltpu
from jax.sharding import PartitionSpec as P

HEAD = 128
TILE = 128
LONGEST = 16
CHUNK = 512
FILL = -1e30
SCALE = math.log2(math.e) / math.sqrt(HEAD)
MESH = pl.DeviceIdType.MESH
EARLY = 11
FIRST = 4


def scores_of(queries, keys):
    return lax.dot_general(
        queries, keys, (((1,), (1,)), ((), ())), preferred_element_type=jnp.float32
    )


def decay(scores, top):
    return jnp.exp2((scores - top) * SCALE)


def attention(units, chunks):
    def score(unit, chunk):
        scores = scores_of(unit(), chunk[0]())
        return scores if chunk[2] is None else jnp.where(chunk[2](), scores, FILL)

    found = []
    ahead = [score(units[0], chunk) for chunk in chunks]
    for at in range(len(units)):
        scores, ahead = ahead, []
        top = functools.reduce(
            jnp.maximum, [jnp.max(s, axis=1, keepdims=True) for s in scores]
        )
        total = acc = 0.0
        for s, chunk in zip(scores, chunks):
            if at + 1 < len(units):
                ahead.append(score(units[at + 1], chunk))
            weights = decay(s, top)
            total = total + jnp.sum(weights, axis=1, keepdims=True)
            acc = acc + jnp.dot(
                weights.astype(jnp.bfloat16), chunk[1](), preferred_element_type=jnp.float32
            )
        found.append((top, total, acc))
    return found


def units_of(q_ref, at, heads):
    return [lambda h=h: q_ref[at, h * HEAD : (h + 1) * HEAD] for h in range(heads)]


def cuts(size):
    return [(start, min(CHUNK, size - start)) for start in range(0, size, CHUNK)]


def prefix_chunks(pre_ref, rows, live):
    keys = pre_ref.shape[1]

    def chunk(start, size):
        def seen():
            return lax.broadcasted_iota(jnp.int32, (rows, size), 1) < live - start

        return (
            lambda: pre_ref[0, start : start + size, :],
            lambda: pre_ref[1, start : start + size, :],
            seen if start + size > keys // 2 else None,
        )

    return [chunk(*cut) for cut in cuts(keys)]


def new_chunk(kv_ref, start, size, seen):
    window = pl.ds(pl.multiple_of(start, HEAD), size)
    return (lambda: kv_ref[0, window, :], lambda: kv_ref[1, window, :], seen)


def document_starts(docs, starts):
    starts[0] = 0

    def begin_of(t):
        starts[t] = jnp.where(docs[0, t] == docs[0, t - 1], starts[t - 1], t)

    each(1, docs.shape[1], begin_of)


def seen_by(starts, block, rows, start, size, causal):
    per = rows // TILE
    tiles = []
    for t in range(per):
        tile = block * per + t
        column = lax.broadcasted_iota(jnp.int32, (TILE, size), 1)
        seen = column >= starts[tile] * TILE - start
        if causal:
            row = lax.broadcasted_iota(jnp.int32, (TILE, size), 0)
            seen = seen & (column - row <= tile * TILE - start)
        tiles.append(seen)
    return jnp.concatenate(tiles, axis=0)


def joined(one, two):
    top = jnp.maximum(one[0], two[0])
    left, right = decay(one[0], top), decay(two[0], top)
    return top, one[1] * left + two[1] * right, one[2] * left + two[2] * right


def pack(columns):
    return jnp.concatenate(
        [jnp.broadcast_to(column, (column.shape[0], HEAD)) for column in columns], axis=1
    )


def part_of(acc_ref, stat_ref, at, h):
    return (
        stat_ref[at, 2 * h * HEAD : (2 * h + 1) * HEAD],
        stat_ref[at, (2 * h + 1) * HEAD : (2 * h + 2) * HEAD],
        acc_ref[at, h * HEAD : (h + 1) * HEAD],
    )


def span(index, size):
    start = index * size
    return pl.ds(start if isinstance(start, int) else pl.multiple_of(start, size), size)


def partner(me, r, columns, sends):
    chips_x = columns // 4
    x, z, core = me // 4, (me // 2) % 2, me % 2
    x = (x + r // 4) % chips_x if sends else (x + chips_x - r // 4) % chips_x
    return x * 4 + ((z + r) % 2) * 2 + (core + r // 2) % 2


def partner_chip(chip, t, chips, sends):
    chips_x = chips // 2
    x, z = chip // 2, chip % 2
    x = (x + t // 2) % chips_x if sends else (x + chips_x - t // 2) % chips_x
    return x * 2 + (z + t) % 2


def each(first, last, act):
    def step(t, c):
        act(t)
        return c

    lax.fori_loop(first, last, step, 0)


def gather_kernel(
    columns, groups, early, wanted_ref, owners_ref, pages, pool_ref, q_ref, new_ref,
    q_all, kv_all, pre_all, acc_ref, stat_ref,
    wanted, owners, pool, outgoing, arrived, staged, req_send, req_recv, q_send, q_recv, kv_send, kv_recv,
    kv_pass, pre_send, pre_recv, pre_pass, near,
):
    me = lax.axis_index("ctx")
    group = lax.axis_index("req")
    chips = columns // 2
    chip = me // 2
    core = me % 2
    sibling = chip * 2 + (1 - core)
    rows = q_ref.shape[0]
    width = q_all.shape[1]
    heads = width // HEAD
    slots, page_len = staged.shape[1], staged.shape[2]
    first = FIRST
    loads = [
        pltpu.make_async_copy(source, here, near.at[3 + i])
        for i, (source, here) in enumerate(
            ((pool_ref, pool), (wanted_ref, wanted), (owners_ref, owners))
        )
    ]
    for load in loads:
        load.start()

    barrier = pltpu.get_barrier_semaphore()

    def greet_column(r):
        to = partner(me, r, columns, True)
        pl.semaphore_signal(barrier, inc=1, device_id={"ctx": to}, device_id_type=MESH)

    def greet_group(t):
        to = (group + t) % groups
        pl.semaphore_signal(barrier, inc=1, device_id={"req": to}, device_id_type=MESH)

    each(1, groups, greet_group)
    each(1, columns, greet_column)
    for load in loads:
        load.wait()
    for g in range(groups):
        outgoing[g] = pool[jnp.maximum(wanted[0, 0, g], 0)]
    arrived[group] = outgoing[group]
    pl.semaphore_wait(barrier, columns + groups - 2)

    def page_copy(t):
        to = (group + t) % groups
        return pltpu.make_async_remote_copy(
            outgoing.at[to], arrived.at[group], req_send.at[t], req_recv.at[group],
            device_id={"req": to}, device_id_type=MESH,
        )

    def q_cut(device):
        return q_ref.at[:, span(device, width)]

    def q_slot(device):
        return q_all.at[span(device, rows), :]

    def kv_slot(device):
        return kv_all.at[:, span(device, rows), :]

    def pre_slot(device):
        return pre_all.at[:, :, device]

    def new_cut(at):
        return new_ref.at[:, :, span(at, HEAD)]

    def pre_cut(at):
        return staged.at[:, :, :, span(at, HEAD)]

    def q_copy(r):
        to = partner(me, r, columns, True)
        return pltpu.make_async_remote_copy(
            q_cut(to), q_slot(me), q_send.at[r], q_recv.at[me],
            device_id={"ctx": to}, device_id_type=MESH,
        )

    def kv_copy(t):
        to = partner_chip(chip, t, chips, True)
        return pltpu.make_async_remote_copy(
            new_cut(to), kv_slot(me), kv_send.at[t], kv_recv.at[me],
            device_id={"ctx": to * 2 + core}, device_id_type=MESH,
        )

    def pre_copy(t):
        to = partner_chip(chip, t, chips, True)
        return pltpu.make_async_remote_copy(
            pre_cut(to), pre_slot(me), pre_send.at[t], pre_recv.at[me],
            device_id={"ctx": to * 2 + core}, device_id_type=MESH,
        )

    def source_of(t):
        return partner_chip(chip, t, chips, False) * 2 + core

    def to_sibling(source_ref, slot, send, recv):
        return pltpu.make_async_remote_copy(
            source_ref, slot, send, recv, device_id={"ctx": sibling}, device_id_type=MESH
        )

    def kv_onward(t):
        slot = kv_slot(source_of(t))
        return to_sibling(slot, slot, kv_pass.at[t], kv_recv.at[source_of(t)])

    def pre_onward(t):
        slot = pre_slot(source_of(t))
        return to_sibling(slot, slot, pre_pass.at[t], pre_recv.at[source_of(t)])

    kv_twin = to_sibling(new_cut(chip), kv_slot(me), kv_pass.at[0], kv_recv.at[me])
    pre_twin = to_sibling(pre_cut(chip), pre_slot(me), pre_pass.at[0], pre_recv.at[me])
    own = [
        pltpu.make_async_copy(q_cut(me), q_slot(me), near.at[0]),
        pltpu.make_async_copy(new_cut(chip), kv_slot(me), near.at[1]),
        pltpu.make_async_copy(pre_cut(chip), pre_slot(me), near.at[2]),
    ]

    each(1, groups, lambda t: page_copy(t).start())
    each(1, first, lambda r: q_copy(r).start())
    own[0].start()
    own[1].start()

    def page_arrival(t):
        source = (group + groups - t) % groups
        pltpu.make_async_remote_copy(
            outgoing.at[source], arrived.at[source], req_send.at[0], req_recv.at[source],
            device_id={"req": source}, device_id_type=MESH,
        ).wait_recv()

    each(1, groups, page_arrival)
    for i in range(slots):
        staged[:, i] = arrived[jnp.maximum(owners[0, 0, i], 0)]
    each(1, chips, lambda t: pre_copy(t).start())
    pre_twin.start()
    own[2].start()
    each(first, early, lambda r: q_copy(r).start())
    each(1, chips, lambda t: kv_copy(t).start())
    kv_twin.start()
    each(early, columns, lambda r: q_copy(r).start())

    def pre_relay(t):
        pre_onward(t).wait_recv()
        pre_onward(t).start()

    each(1, chips, pre_relay)

    def pre_twin_arrival(t):
        source = partner_chip(chip, t, chips, False) * 2 + (1 - core)
        to_sibling(pre_slot(source), pre_slot(source), near.at[3], pre_recv.at[source]).wait_recv()

    each(0, chips, pre_twin_arrival)
    own[0].wait()
    own[2].wait()
    keys = slots * columns * page_len
    live = pages[0] * page_len
    prefix = pre_all.reshape(2, keys, HEAD)

    def q_arrival(r):
        source = partner(me, r, columns, False)
        pltpu.make_async_remote_copy(
            q_slot(source), q_slot(source), q_send.at[0], q_recv.at[source],
            device_id={"ctx": source}, device_id_type=MESH,
        ).wait_recv()

    def attend(r):
        at = span(partner(me, r, columns, False), rows)
        out = span(r, rows)
        parts = attention(units_of(q_all, at, heads), prefix_chunks(prefix, rows, live))
        for h, part in enumerate(parts):
            acc_ref[out, h * HEAD : (h + 1) * HEAD] = part[2]
        stat_ref[out, :] = pack([column for part in parts for column in part[:2]])

    attend(0)

    def arrive_and_attend(r):
        q_arrival(r)
        attend(r)

    each(1, early, arrive_and_attend)

    def kv_relay(t):
        kv_onward(t).wait_recv()
        kv_onward(t).start()

    each(1, chips, kv_relay)
    each(early, columns, q_arrival)

    def kv_twin_arrival(t):
        source = partner_chip(chip, t, chips, False) * 2 + (1 - core)
        to_sibling(kv_slot(source), kv_slot(source), near.at[3], kv_recv.at[source]).wait_recv()

    each(0, chips, kv_twin_arrival)
    each(1, groups, lambda t: page_copy(t).wait_send())
    each(1, columns, lambda r: q_copy(r).wait_send())
    for copies in (kv_copy, pre_copy, kv_onward, pre_onward):
        each(1, chips, lambda t, copies=copies: copies(t).wait_send())
    kv_twin.wait_send()
    pre_twin.wait_send()
    own[1].wait()


def in_hbm(x):
    return pltpu.with_memory_space_constraint(x, pltpu.HBM)


def gather(wanted, owners, pages, pool, queries, kv_new, columns, groups, early):
    rows, features = queries.shape
    slots, page_len = owners.shape[2], pool.shape[2]
    dtype = queries.dtype
    width = features // columns
    dma = pltpu.SemaphoreType.DMA
    smem = pl.BlockSpec(memory_space=pltpu.SMEM)
    vmem = pl.BlockSpec(memory_space=pltpu.VMEM)
    hbm = pl.BlockSpec(memory_space=pltpu.HBM)
    chips = columns // 2
    return pl.pallas_call(
        lambda *refs: gather_kernel(columns, groups, early, *refs),
        out_shape=(
            jax.ShapeDtypeStruct((rows * columns, width), dtype),
            jax.ShapeDtypeStruct((2, rows * columns, HEAD), dtype),
            jax.ShapeDtypeStruct((2, slots, columns, page_len, HEAD), dtype),
            jax.ShapeDtypeStruct((rows * early, width), jnp.float32),
            jax.ShapeDtypeStruct((rows * early, 2 * width), jnp.float32),
        ),
        in_specs=[hbm, hbm, smem, hbm, hbm, hbm],
        out_specs=(vmem, vmem, vmem, vmem, vmem),
        scratch_shapes=[
            pltpu.SMEM(wanted.shape, jnp.int32),
            pltpu.SMEM(owners.shape, jnp.int32),
            pltpu.VMEM(pool.shape, dtype),
            pltpu.VMEM((groups,) + pool.shape[1:], dtype),
            pltpu.VMEM((groups,) + pool.shape[1:], dtype),
            pltpu.VMEM((2, slots) + pool.shape[2:], dtype),
            dma((groups,)), dma((groups,)),
            dma((columns,)), dma((columns,)),
            dma((chips,)), dma((columns,)), dma((chips,)),
            dma((chips,)), dma((columns,)), dma((chips,)),
            dma((6,)),
        ],
        compiler_params=pltpu.CompilerParams(
            collective_id=0, has_side_effects=True, vmem_limit_bytes=32 << 20
        ),
        name="gather",
    )(
        in_hbm(wanted), in_hbm(owners), pages, in_hbm(pool), in_hbm(queries), in_hbm(kv_new)
    )


def new_kernel(columns, docs, q_ref, kv_ref, acc_pre, stat_pre, done_ref, acc_s, stat_s, starts):
    me = lax.axis_index("ctx")
    rows, width = acc_s.shape
    heads = width // HEAD
    per = rows // TILE
    document_starts(docs, starts)

    def do(slot):
        block = partner(me, slot, columns, False)
        begin = starts[block * per] // per
        at = span(block, rows)

        def fold(before):
            def chunk(start, size, causal):
                seen = lambda: seen_by(starts, block, rows, start, size, causal)
                return new_chunk(kv_ref, start, size, seen)

            chunks = [chunk(begin * rows + at, size, False) for at, size in cuts(before * rows)]
            chunks.append(chunk(block * rows, rows, True))
            parts = attention(units_of(q_ref, at, heads), chunks)
            for h, part in enumerate(parts):
                acc_s[:, h * HEAD : (h + 1) * HEAD] = part[2]
            stat_s[...] = pack([column for part in parts for column in part[:2]])

        for before in range(LONGEST // per + 1):
            pl.when(block - begin == before)(lambda before=before: fold(before))

        here = span(slot, rows)
        for h in range(heads):
            _, total, acc = joined(
                part_of(acc_s, stat_s, slice(None), h), part_of(acc_pre, stat_pre, here, h)
            )
            done_ref[here, h * HEAD : (h + 1) * HEAD] = (acc / total).astype(done_ref.dtype)

    each(0, done_ref.shape[0] // rows, do)


def attend_new(docs, queries, kv, acc, stat, rows):
    positions, width = queries.shape
    smem = pl.BlockSpec(memory_space=pltpu.SMEM)
    vmem = pl.BlockSpec(memory_space=pltpu.VMEM)
    return pl.pallas_call(
        lambda *refs: new_kernel(positions // rows, *refs),
        out_shape=jax.ShapeDtypeStruct(acc.shape, queries.dtype),
        in_specs=[smem, vmem, vmem, vmem, vmem],
        out_specs=vmem,
        scratch_shapes=[
            pltpu.VMEM((rows, width), jnp.float32),
            pltpu.VMEM((rows, 2 * width), jnp.float32),
            pltpu.SMEM((docs.shape[1],), jnp.int32),
        ],
        compiler_params=pltpu.CompilerParams(vmem_limit_bytes=40 << 20),
        name="attend_new",
    )(docs, queries, kv, acc, stat)


def finish_kernel(
    columns, pages, docs, q_ref, pre_ref, kv_ref, done_ref, out_ref, stage, starts, send, recv, near
):
    me = lax.axis_index("ctx")
    positions, width = q_ref.shape
    rows = positions // columns
    heads = width // HEAD
    early = done_ref.shape[0] // rows
    live = pages[0] * (pre_ref.shape[1] // 64)

    barrier = pltpu.get_barrier_semaphore()

    def greet(r):
        to = partner(me, r, columns, False)
        pl.semaphore_signal(barrier, inc=1, device_id={"ctx": to}, device_id_type=MESH)

    each(1, columns, greet)
    document_starts(docs, starts)
    pl.semaphore_wait(barrier, columns - 1)

    def cut_of(device):
        return out_ref.at[:, span(device, width)]

    def send_block(source, r):
        to = partner(me, r, columns, False)
        return pltpu.make_async_remote_copy(
            source, cut_of(me), send.at[r], recv.at[me], device_id={"ctx": to}, device_id_type=MESH
        )

    each(1, early, lambda r: send_block(done_ref.at[span(r, rows), :], r).start())
    mine = pltpu.make_async_copy(done_ref.at[0:rows, :], cut_of(me), near)
    mine.start()
    longest = LONGEST * TILE // rows

    def late(i):
        block = partner(me, early + i, columns, False)
        begin = jnp.maximum(block - longest, 0) * rows

        def chunk(offset, size):
            start = begin + offset
            seen = lambda: seen_by(starts, block, rows, start, size, True)
            return new_chunk(kv_ref, start, size, seen)

        chunks = prefix_chunks(pre_ref, rows, live)
        chunks += [chunk(*cut) for cut in cuts((longest + 1) * rows)]
        here = span(i, rows)
        for h, part in enumerate(attention(units_of(q_ref, span(block, rows), heads), chunks)):
            stage[here, h * HEAD : (h + 1) * HEAD] = (part[2] / part[1]).astype(stage.dtype)
        send_block(stage.at[here, :], early + i).start()

    each(0, columns - early, late)

    def settle(r):
        source = partner(me, r, columns, True)
        pltpu.make_async_remote_copy(
            done_ref.at[0:rows, :], cut_of(source), send.at[0], recv.at[source],
            device_id={"ctx": source}, device_id_type=MESH,
        ).wait_recv()
        send_block(done_ref.at[0:rows, :], r).wait_send()

    each(1, columns, settle)
    mine.wait()


def finish(pages, docs, queries, pre, kv, done, columns):
    positions, width = queries.shape
    smem = pl.BlockSpec(memory_space=pltpu.SMEM)
    vmem = pl.BlockSpec(memory_space=pltpu.VMEM)
    return pl.pallas_call(
        lambda *refs: finish_kernel(columns, *refs),
        out_shape=jax.ShapeDtypeStruct((positions // columns, width * columns), queries.dtype),
        in_specs=[smem, smem, vmem, vmem, vmem, vmem],
        out_specs=pl.BlockSpec(memory_space=pl.ANY),
        scratch_shapes=[
            pltpu.VMEM((positions - done.shape[0], width), queries.dtype),
            pltpu.SMEM((docs.shape[1],), jnp.int32),
            pltpu.SemaphoreType.DMA((columns,)),
            pltpu.SemaphoreType.DMA((columns,)),
            pltpu.SemaphoreType.DMA,
        ],
        compiler_params=pltpu.CompilerParams(
            collective_id=1, has_side_effects=True, vmem_limit_bytes=40 << 20
        ),
        name="finish",
    )(pages, docs, queries, pre, kv, done)


def local(queries, kv_new, kv_pool, prefix_pages, reader_owner, send_page, tile_doc):
    columns, groups = lax.axis_size("ctx"), lax.axis_size("req")
    q, kv, pre, acc, stat = gather(
        send_page, reader_owner, prefix_pages, kv_pool, queries[0], kv_new[0], columns, groups, EARLY
    )
    done = attend_new(tile_doc, q, kv, acc, stat, queries.shape[1])
    return finish(prefix_pages, tile_doc, q, pre.reshape(2, -1, HEAD), kv, done, columns)[None]


def solution(mesh):
    in_specs = (
        P("req", "ctx", None),
        P("req", None, "ctx", None),
        P(("req", "ctx"), None, None, None),
        P("req"),
        P("req", "ctx", None),
        P("req", "ctx", None),
        P("req", None),
    )
    return jax.shard_map(
        local, mesh=mesh, in_specs=in_specs, out_specs=P("req", "ctx", None), check_vma=False
    )
```
